128 devices in a mesh: inp: 16 (over y, z_lo, core), tm: 8 (over z_hi, x).
Axes of the slice: x: 4, y: 4, z: 4 (z_hi: 2, z_lo: 2; z = z_hi * 2 + z_lo), core: 2. Of those that a mesh axis runs over, the one named last changes fastest.
Arguments:
- voltages: bfloat16 [1024, 524288], P('inp', 'tm'), may hold values from -6 to 6
- prototype: float32 [8, 1024], replicated, may hold values from -2 to 2
Outputs:
- correlation: bfloat16 [512, 2, 1024, 1024], P(('inp', 'tm'))
The draws below stay inside these ranges and needn't reach their ends.
All inputs are finite; a program needn't handle non-finite values.
Results may differ from the reference program's by a relative error of at most 0.0065.
Values may be sent and summed in bfloat16 or wider, within the bound.
A program may use at most 128 MiB of HBM per device.

```python
import math
import jax
import jax.numpy as jnp
from jax import lax

INPUTS = 1024
CHAN = 512
TAPS = 8
FRAME = 1024
SPEC = 512
SAMPLES = 524288


def levels(key, shape, pieces, least, top_value):
    level, own = 1.0, jax.random.fold_in(key, 6)
    for axis_at, blocks in pieces:
        steps = jnp.exp(jax.random.uniform(jax.random.fold_in(own, axis_at), (blocks,), jnp.float32, least / len(pieces), top_value / len(pieces)))
        level = level * jnp.repeat(steps, shape[axis_at] // blocks).reshape([-1 if axis == axis_at else 1 for axis in range(len(shape))])
    return level


def gaussian(stream_key, extent, spread, bound, cuts=(), kind=jnp.bfloat16):
    array = jax.random.normal(stream_key, extent, jnp.float32) * spread
    if len(cuts) > 0:
        array = levels(stream_key, extent, cuts, -0.22, 0.18) * array
    return jnp.clip(array, min=-bound, max=bound).astype(kind)


def setup_inputs(seed: int = 0) -> dict:
    keys = jax.random.split(jax.random.key(seed), 3)
    voltages = gaussian(keys[0], (INPUTS, SAMPLES), 1.0, 6.0, ((0, 16), (1, 8)))
    prototype = gaussian(keys[1], (TAPS, FRAME), 0.35, 2.0, (), jnp.float32)
    return dict(voltages=voltages, prototype=prototype)


def dft_table(frame):
    sample = jnp.arange(frame, dtype=jnp.int32)[:, None]
    column = jnp.arange(frame, dtype=jnp.int32)[None, :]
    phase = (sample * (column // 2) % frame).astype(jnp.float32) * (2.0 * math.pi / frame)
    table = jnp.where(column % 2 == 0, jnp.cos(phase), -jnp.sin(phase))
    return table.astype(jnp.bfloat16)

def channelize(frames, earlier, prototype):
    count = frames.shape[1]
    joined = jnp.concatenate([earlier, frames], axis=1)
    filtered = jnp.zeros(frames.shape, jnp.float32)
    for tap_index in range(TAPS):
        filtered = filtered + prototype[tap_index] * joined[:, tap_index:tap_index + count, :].astype(jnp.float32)
    filtered = filtered.astype(jnp.bfloat16)
    flat = filtered.reshape(-1, frames.shape[2])
    spectra = jnp.dot(flat, dft_table(frames.shape[2]), preferred_element_type=jnp.float32)
    return spectra.astype(jnp.bfloat16).reshape(frames.shape)

def correlate(planes):
    real_part = planes[0]
    imag_part = planes[1]
    left = jnp.concatenate([real_part, imag_part], axis=1)
    right = jnp.concatenate([imag_part, -real_part], axis=1)
    dims = (((1,), (1,)), ((), ()))
    real_gram = lax.dot_general(left, left, dims, preferred_element_type=jnp.float32)
    imag_gram = lax.dot_general(right, left, dims, preferred_element_type=jnp.float32)
    scales = lax.rsqrt(jnp.diagonal(real_gram) + 1e-06)
    outer = scales[:, None] * scales[None, :]
    return jnp.stack([real_gram * outer, imag_gram * outer]).astype(jnp.bfloat16)

def reference(voltages, prototype):
    block = math.gcd(INPUTS, 64)
    grouped = voltages.reshape(INPUTS // block, block, SPEC, FRAME)

    def one_block(frames):
        earlier = jnp.zeros((block, TAPS - 1, FRAME), jnp.bfloat16)
        return channelize(frames, earlier, prototype)
    spectra = lax.map(one_block, grouped).reshape(INPUTS, SPEC, CHAN, 2)
    planes = spectra.transpose(2, 3, 0, 1)
    return lax.map(correlate, planes)
```

```python
import functools
import math

import jax
import jax.numpy as jnp
import numpy as np
from jax import lax
from jax.experimental import pallas as pl
from jax.experimental.pallas import tpu as pltpu
from jax.sharding import PartitionSpec as P

TAPS = 8
HALO = TAPS - 1
FRAME = 1024
INPUTS_DEV = 64
SPEC_DEV = 64
DEVICES = 128
GROUPS = 4
INP = 16
TM = 8
PAIRS = SPEC_DEV // 2
MESH = pl.DeviceIdType.MESH


def dft_rows():
    channel = np.arange(DEVICES)[None, :] * GROUPS + np.arange(GROUPS)[:, None]
    sample = np.arange(FRAME)
    phase = (channel[:, :, None] * sample % FRAME) * (2.0 * math.pi / FRAME)
    table = np.stack([np.cos(phase), -np.sin(phase)], axis=2)
    return table.reshape(GROUPS, 2 * DEVICES, FRAME).astype(jnp.bfloat16)


def channelize_kernel(
    v_hbm, proto_ref, table_hbm, r_hbm,
    v, table, filtered, turned, outbox,
    v_sem, table_sem, own_sem, halo_sems, send_sems, recv_sems,
):
    a = lax.axis_index("inp")
    b = lax.axis_index("tm")
    me = a * TM + b
    barrier = pltpu.get_barrier_semaphore()

    def place(k):
        other = lax.rem(me + k, DEVICES)
        return other, {"inp": other // TM, "tm": lax.rem(other, TM)}

    @pl.loop(1, DEVICES)
    def _(k):
        _, where = place(k)
        pl.semaphore_signal(barrier, inc=1, device_id=where, device_id_type=MESH)

    body = HALO * FRAME
    loads = [
        pltpu.make_async_copy(
            v_hbm.at[pl.ds(q * 16, 16), :],
            v.at[pl.ds(q * 16, 16), pl.ds(body, SPEC_DEV * FRAME)],
            v_sem.at[q],
        )
        for q in range(4)
    ]
    for load in loads:
        load.start()
    table_load = pltpu.make_async_copy(table_hbm, table, table_sem)
    table_load.start()

    def fir(q, chunk):
        @pl.loop(0, FRAME // 128)
        def _(nb):
            lanes = pl.multiple_of(nb * 128, 128)
            taps = [proto_ref[k : k + 1, pl.ds(lanes, 128)] for k in range(TAPS)]
            x = [
                v[
                    pl.ds(q * 16, 16),
                    pl.ds(pl.multiple_of((chunk * 8 + f) * FRAME + lanes, 128), 128),
                ].astype(jnp.float32)
                for f in range(8 + HALO)
            ]
            for s in range(8):
                total = taps[0] * x[s]
                for k in range(1, TAPS):
                    total = total + taps[k] * x[s + k]
                filtered[chunk * 8 + s, pl.ds(q * 16, 16), pl.ds(lanes, 128)] = total.astype(
                    jnp.bfloat16
                )

    halo = pltpu.make_async_remote_copy(
        src_ref=v_hbm.at[:, pl.ds((SPEC_DEV - HALO) * FRAME, body)],
        dst_ref=v.at[:, pl.ds(0, body)],
        send_sem=halo_sems.at[0],
        recv_sem=halo_sems.at[1],
        device_id={"tm": lax.rem(b + 1, TM)},
        device_id_type=MESH,
    )
    for q in range(4):
        loads[q].wait()
        pl.loop(1, 8)(functools.partial(fir, q))
        if q == 0:
            pl.semaphore_wait(barrier, DEVICES - 1)

            @pl.when(b < TM - 1)
            def _():
                halo.start()

    @pl.when(b == 0)
    def _():
        @pl.loop(0, HALO)
        def _(f):
            v[:, pl.ds(pl.multiple_of(f * FRAME, FRAME), FRAME)] = jnp.zeros(
                (INPUTS_DEV, FRAME), jnp.bfloat16
            )

    @pl.when(b > 0)
    def _():
        halo.wait_recv()

    for q in range(4):
        fir(q, 0)
    table_load.wait()

    @pl.loop(0, GROUPS)
    def _(j):
        rows = table.at[j]

        @pl.loop(0, 8)
        def _(cb):
            block = filtered[pl.ds(cb * 8, 8)].reshape(8 * INPUTS_DEV, FRAME)
            out = lax.dot_general(
                rows[...], block, (((1,), (1,)), ((), ())), preferred_element_type=jnp.float32
            )
            for l in range(4):
                turned[pl.ds(cb * 4 + l, 2 * DEVICES, stride=PAIRS), :] = out[
                    :, l * 128 : (l + 1) * 128
                ]

        @pl.loop(0, 32)
        def _(r):
            outbox[j, pl.ds(r * 4, 4)] = (
                turned[pl.ds(pl.multiple_of(r * 256, 256), 256), :]
                .astype(jnp.bfloat16)
                .reshape(4, 2, PAIRS, 128)
            )

        pltpu.make_async_copy(
            outbox.at[j, me], r_hbm.at[j, a, :, pl.ds(b * PAIRS, PAIRS), :], own_sem.at[j]
        ).start()

        @pl.loop(1, DEVICES)
        def _(k):
            other, where = place(k)
            pltpu.make_async_remote_copy(
                src_ref=outbox.at[j, other],
                dst_ref=r_hbm.at[j, a, :, pl.ds(b * PAIRS, PAIRS), :],
                send_sem=send_sems.at[j],
                recv_sem=recv_sems.at[j],
                device_id=where,
                device_id_type=MESH,
            ).start()

    @pl.when(b < TM - 1)
    def _():
        halo.wait_send()

    @pl.loop(0, GROUPS)
    def _(j):
        pltpu.make_async_copy(
            outbox.at[j, me], r_hbm.at[j, a, :, pl.ds(b * PAIRS, PAIRS), :], own_sem.at[j]
        ).wait()
        sent = outbox.at[j, pl.ds(0, DEVICES - 1)]
        pltpu.make_async_copy(sent, sent, send_sems.at[j]).wait()
        pltpu.make_async_copy(sent, sent, recv_sems.at[j]).wait()


def channelize(voltages, prototype, table):
    return pl.pallas_call(
        channelize_kernel,
        out_shape=jax.ShapeDtypeStruct((GROUPS, INP, 2, TM * PAIRS, 128), jnp.bfloat16),
        in_specs=[
            pl.BlockSpec(memory_space=pl.ANY),
            pl.BlockSpec(memory_space=pltpu.VMEM),
            pl.BlockSpec(memory_space=pl.ANY),
        ],
        out_specs=pl.BlockSpec(memory_space=pl.ANY),
        scratch_shapes=[
            pltpu.VMEM((INPUTS_DEV, (SPEC_DEV + HALO) * FRAME), jnp.bfloat16),
            pltpu.VMEM((GROUPS, 2 * DEVICES, FRAME), jnp.bfloat16),
            pltpu.VMEM((SPEC_DEV, INPUTS_DEV, FRAME), jnp.bfloat16),
            pltpu.VMEM((2 * DEVICES * PAIRS, 128), jnp.float32),
            pltpu.VMEM((GROUPS, DEVICES, 2, PAIRS, 128), jnp.bfloat16),
            pltpu.SemaphoreType.DMA((4,)),
            pltpu.SemaphoreType.DMA,
            pltpu.SemaphoreType.DMA((GROUPS,)),
            pltpu.SemaphoreType.DMA((2,)),
            pltpu.SemaphoreType.DMA((GROUPS,)),
            pltpu.SemaphoreType.DMA((GROUPS,)),
        ],
        compiler_params=pltpu.CompilerParams(
            collective_id=0, has_side_effects=True, vmem_limit_bytes=56 * 1024 * 1024
        ),
        name="channelize",
    )(voltages, prototype, table)


def correlate_kernel(r_ref, o_ref, y, yt, scale_col, scale_row):
    step = pl.program_id(1)
    half = TM * PAIRS

    @pl.when(step == 0)
    def _():
        low = lax.broadcasted_iota(jnp.int32, (half, 128), 1) < 64
        for q in range(INP // 2):
            power = jnp.zeros((1, 128), jnp.float32)
            for p in range(2):
                even = r_ref[0, 2 * q, p].astype(jnp.float32)
                odd = r_ref[0, 2 * q + 1, p].astype(jnp.float32)
                first = jnp.where(low, even, pltpu.roll(odd, 64, 1))
                second = jnp.where(low, pltpu.roll(even, 64, 1), odd)
                power = power + jnp.sum(first * first + second * second, axis=0, keepdims=True)
                for h, part in enumerate((first, second)):
                    part = part.astype(jnp.bfloat16)
                    base = (2 * p + h) * half
                    y[base : base + half, q * 128 : (q + 1) * 128] = part
                    yt[q * 128 : (q + 1) * 128, base : base + half] = part.T
            scale = lax.rsqrt(power + 1e-06)
            scale_row[:, q * 128 : (q + 1) * 128] = scale
            scale_col[q * 128 : (q + 1) * 128, :] = jnp.broadcast_to(scale, (128, 128)).T

    rows = pl.ds(pl.multiple_of(step * 256, 256), 256)
    left = yt[rows, :]
    right = jnp.concatenate([left[:, 2 * half :], -left[:, : 2 * half]], axis=1)
    column = scale_col[rows, 0:1]
    for n in range(4):
        cols = slice(n * 256, (n + 1) * 256)
        outer = column * scale_row[:, cols]
        gram = jnp.dot(left, y[:, cols], preferred_element_type=jnp.float32)
        o_ref[0, 0, :, cols] = (gram * outer).astype(jnp.bfloat16)
        gram = jnp.dot(right, y[:, cols], preferred_element_type=jnp.float32)
        o_ref[0, 1, :, cols] = (gram * outer).astype(jnp.bfloat16)


def correlate(received):
    return pl.pallas_call(
        correlate_kernel,
        grid=(GROUPS, 4),
        out_shape=jax.ShapeDtypeStruct((GROUPS, 2, 1024, 1024), jnp.bfloat16),
        in_specs=[
            pl.BlockSpec((1, INP, 2, TM * PAIRS, 128), lambda c, i: (c, 0, 0, 0, 0)),
        ],
        out_specs=pl.BlockSpec((1, 2, 256, 1024), lambda c, i: (c, 0, i, 0)),
        scratch_shapes=[
            pltpu.VMEM((1024, 1024), jnp.bfloat16),
            pltpu.VMEM((1024, 1024), jnp.bfloat16),
            pltpu.VMEM((1024, 128), jnp.float32),
            pltpu.VMEM((1, 1024), jnp.float32),
        ],
        compiler_params=pltpu.CompilerParams(vmem_limit_bytes=48 * 1024 * 1024),
        name="correlate",
    )(received)


def shards(voltages, prototype):
    table = jnp.asarray(dft_rows())
    return correlate(channelize(voltages, prototype, table))


def solution(mesh):
    return jax.shard_map(
        shards,
        mesh=mesh,
        in_specs=(P("inp", "tm"), P()),
        out_specs=P(("inp", "tm"), None, None, None),
        check_vma=False,
    )
```

```python
import functools
import math

import jax
import jax.numpy as jnp
import numpy as np
from jax import lax
from jax.experimental import pallas as pl
from jax.experimental.pallas import tpu as pltpu
from jax.sharding import PartitionSpec as P

TAPS = 8
HALO = TAPS - 1
FRAME = 1024
INPUTS = 1024
INPUTS_DEV = 64
SPEC_DEV = 64
DEVICES = 128
GROUPS = 4
INP = 16
TM = 8
HALF = SPEC_DEV // 2
PAIRS = HALF // 2
STRIDE = PAIRS + 1
TILE = 256
MESH = pl.DeviceIdType.MESH


def dft_rows():
    channel = np.arange(DEVICES)[None, :] * GROUPS + np.arange(GROUPS)[:, None]
    sample = np.arange(FRAME)
    phase = (channel[:, :, None] * sample % FRAME) * (2.0 * math.pi / FRAME)
    table = np.stack([np.cos(phase), -np.sin(phase)], axis=2)
    return table.reshape(GROUPS, 2 * DEVICES, FRAME).astype(jnp.bfloat16)


def correlate_channel(received, rows, scale_col, scale_row, out):
    @pl.loop(0, INP)
    def _(a):
        at = pl.ds(pl.multiple_of(a * INPUTS_DEV, INPUTS_DEV), INPUTS_DEV)
        for p in range(2):
            turned = received[a, :, :, p].reshape(TM * HALF, 128).T
            for h in range(2):
                base = (2 * p + h) * TM * HALF
                rows[at, base : base + TM * HALF] = turned[h * 64 : (h + 1) * 64]

    half = INPUTS // 2

    def grams(left, right, n):
        other = rows[n * TILE : (n + 1) * TILE, :]
        dims = (((1,), (1,)), ((), ()))
        return (
            lax.dot_general(left, other, dims, preferred_element_type=jnp.float32),
            lax.dot_general(right, other, dims, preferred_element_type=jnp.float32),
        )

    def sides(m):
        left = rows[m * TILE : (m + 1) * TILE, :]
        return left, jnp.concatenate([left[:, half:], -left[:, :half]], axis=1)

    eye = lax.broadcasted_iota(jnp.int32, (TILE, TILE), 0) == lax.broadcasted_iota(
        jnp.int32, (TILE, TILE), 1
    )
    for m in range(INPUTS // TILE):
        at = slice(m * TILE, (m + 1) * TILE)
        real, imag = grams(*sides(m), m)
        diagonal = jnp.where(eye, real, 0.0)
        column = lax.rsqrt(jnp.sum(diagonal, axis=1, keepdims=True) + 1e-06)
        row = lax.rsqrt(jnp.sum(diagonal, axis=0, keepdims=True) + 1e-06)
        scale_col[at, :] = jnp.broadcast_to(column, (TILE, 128))
        scale_row[:, at] = row
        outer = column * row
        out[0, at, at] = (real * outer).astype(jnp.bfloat16)
        out[1, at, at] = (imag * outer).astype(jnp.bfloat16)
    for m in range(INPUTS // TILE - 1):
        left, right = sides(m)
        at = slice(m * TILE, (m + 1) * TILE)
        column = scale_col[at, 0:1]
        for n in range(m + 1, INPUTS // TILE):
            to = slice(n * TILE, (n + 1) * TILE)
            outer = column * scale_row[:, to]
            real, imag = grams(left, right, n)
            real = (real * outer).astype(jnp.bfloat16)
            imag = (imag * outer).astype(jnp.bfloat16)
            out[0, at, to] = real
            out[1, at, to] = imag
            out[0, to, at] = real.T
            out[1, to, at] = -imag.T


def channelize_kernel(
    v_hbm, proto_ref, table_hbm, done_hbm, last_hbm,
    v, table, filtered, turned, outbox, inbox, rows, scale_col, scale_row, staged,
    v_sems, table_sem, own_sems, halo_sems, send_sems, recv_sems, done_sems,
):
    a = lax.axis_index("inp")
    b = lax.axis_index("tm")
    me = a * TM + b
    barrier = pltpu.get_barrier_semaphore()
    body = HALO * FRAME
    split = HALF * FRAME

    loads = [
        pltpu.make_async_copy(
            v_hbm.at[:, pl.ds(split - body, SPEC_DEV * FRAME - split + body)],
            v.at[:, pl.ds(split, SPEC_DEV * FRAME - split + body)],
            v_sems.at[1],
        ),
        pltpu.make_async_copy(
            v_hbm.at[:, pl.ds(0, split - body)], v.at[:, pl.ds(body, split - body)], v_sems.at[0]
        ),
    ]
    table_load = pltpu.make_async_copy(table_hbm, table, table_sem)
    loads[0].start()
    table_load.start()
    loads[1].start()

    def place(k):
        other = lax.rem(me + k * 37, DEVICES)
        return other, {"inp": lax.div(other, TM), "tm": lax.rem(other, TM)}

    @pl.loop(1, DEVICES)
    def _(k):
        _, where = place(k)
        pl.semaphore_signal(barrier, inc=1, device_id=where, device_id_type=MESH)

    def fir(t):
        chunk = lax.div(t, 4)
        at = pl.ds(pl.multiple_of(lax.rem(t, 4) * 16, 16), 16)
        for nb in range(FRAME // 128):
            lanes = slice(nb * 128, (nb + 1) * 128)
            taps = [proto_ref[k : k + 1, lanes] for k in range(TAPS)]
            x = [
                v[
                    at, pl.ds(pl.multiple_of((chunk * 8 + f) * FRAME + nb * 128, 128), 128)
                ].astype(jnp.float32)
                for f in range(8 + HALO)
            ]
            for s in range(8):
                total = taps[0] * x[s]
                for k in range(1, TAPS):
                    total = total + taps[k] * x[s + k]
                filtered[chunk * 8 + s, at, lanes] = total.astype(jnp.bfloat16)

    def dft(j, half):
        block = filtered[pl.ds(half * HALF, HALF)].reshape(HALF * INPUTS_DEV, FRAME)
        out = lax.dot_general(
            table[j], block, (((1,), (1,)), ((), ())), preferred_element_type=jnp.float32
        )
        for l in range(PAIRS):
            turned[pl.ds(l, 2 * DEVICES, stride=STRIDE), :] = out[:, l * 128 : (l + 1) * 128]
        for m in range(2 * DEVICES):
            outbox[j, m // 2, half, m % 2] = turned[pl.ds(m * STRIDE, PAIRS), :].astype(
                jnp.bfloat16
            )

    def send(j, source, target):
        @pl.loop(1, DEVICES)
        def _(k):
            other, where = place(k)
            pltpu.make_async_remote_copy(
                src_ref=source(other),
                dst_ref=target,
                send_sem=send_sems.at[j],
                recv_sem=recv_sems.at[j],
                device_id=where,
                device_id_type=MESH,
            ).start()

    halo = pltpu.make_async_remote_copy(
        src_ref=v_hbm.at[:, pl.ds((SPEC_DEV - HALO) * FRAME, body)],
        dst_ref=v.at[:, pl.ds(0, body)],
        send_sem=halo_sems.at[0],
        recv_sem=halo_sems.at[1],
        device_id={"tm": lax.rem(b + 1, TM)},
        device_id_type=MESH,
    )

    loads[0].wait()
    pl.loop(16, 32)(fir)
    table_load.wait()

    @pl.loop(0, 2)
    def _(j):
        dft(j, 1)

        @pl.when(j == 0)
        def _():
            pl.semaphore_wait(barrier, DEVICES - 1)

            @pl.when(b < TM - 1)
            def _():
                halo.start()

        send(j, lambda other: outbox.at[j, other, 1], inbox.at[j, a, b, 1])

    loads[1].wait()
    pl.loop(4, 16)(fir)

    @pl.when(b == 0)
    def _():
        @pl.loop(0, HALO)
        def _(f):
            v[:, pl.ds(pl.multiple_of(f * FRAME, FRAME), FRAME)] = jnp.zeros(
                (INPUTS_DEV, FRAME), jnp.bfloat16
            )

    @pl.when(b > 0)
    def _():
        halo.wait_recv()

    pl.loop(0, 4)(fir)

    @pl.loop(0, 2)
    def _(j):
        dft(j, 0)
        send(j, lambda other: outbox.at[j, other, 0], inbox.at[j, a, b, 0])

    @pl.loop(2, GROUPS)
    def _(j):
        @pl.loop(0, 2)
        def _(half):
            dft(j, half)

        @pl.when(j == 2)
        def _():
            send(2, lambda other: outbox.at[2, other], inbox.at[2, a, b])

        @pl.when(j == 3)
        def _():
            send(3, lambda other: outbox.at[3, other], last_hbm.at[a, b])

    owns = [
        pltpu.make_async_copy(
            outbox.at[j, me], inbox.at[j, a, b] if j < 3 else last_hbm.at[a, b], own_sems.at[j]
        )
        for j in range(GROUPS)
    ]
    for own in owns:
        own.start()

    @pl.when(b < TM - 1)
    def _():
        halo.wait_send()

    def arrived(j):
        some = outbox.at[j, pl.ds(0, DEVICES - 1)]
        pltpu.make_async_copy(some, some, recv_sems.at[j]).wait()

    def written(j):
        return pltpu.make_async_copy(staged.at[lax.rem(j, 2)], done_hbm.at[j], done_sems.at[j])

    for j in range(3):
        owns[j].wait()

    @pl.loop(0, 3)
    def _(j):
        arrived(j)

        @pl.when(j == 2)
        def _():
            written(0).wait()

        correlate_channel(inbox.at[j], rows, scale_col, scale_row, staged.at[lax.rem(j, 2)])
        written(j).start()

    written(1).wait()
    written(2).wait()
    owns[3].wait()
    arrived(3)

    @pl.loop(0, GROUPS)
    def _(j):
        some = outbox.at[j, pl.ds(0, DEVICES - 1)]
        pltpu.make_async_copy(some, some, send_sems.at[j]).wait()


def channelize(voltages, prototype, table):
    piece = (INP, TM, 2, 2, PAIRS, 128)
    return pl.pallas_call(
        channelize_kernel,
        out_shape=(
            jax.ShapeDtypeStruct((3, 2, INPUTS, INPUTS), jnp.bfloat16),
            jax.ShapeDtypeStruct(piece, jnp.bfloat16),
        ),
        in_specs=[
            pl.BlockSpec(memory_space=pl.ANY),
            pl.BlockSpec(memory_space=pltpu.VMEM),
            pl.BlockSpec(memory_space=pl.ANY),
        ],
        out_specs=(pl.BlockSpec(memory_space=pl.ANY), pl.BlockSpec(memory_space=pl.ANY)),
        scratch_shapes=[
            pltpu.VMEM((INPUTS_DEV, (SPEC_DEV + HALO) * FRAME), jnp.bfloat16),
            pltpu.VMEM((GROUPS, 2 * DEVICES, FRAME), jnp.bfloat16),
            pltpu.VMEM((SPEC_DEV, INPUTS_DEV, FRAME), jnp.bfloat16),
            pltpu.VMEM((2 * DEVICES * STRIDE, 128), jnp.float32),
            pltpu.VMEM((GROUPS, DEVICES, 2, 2, PAIRS, 128), jnp.bfloat16),
            pltpu.VMEM((3, *piece), jnp.bfloat16),
            pltpu.VMEM((INPUTS, INPUTS), jnp.bfloat16),
            pltpu.VMEM((INPUTS, 128), jnp.float32),
            pltpu.VMEM((1, INPUTS), jnp.float32),
            pltpu.VMEM((2, 2, INPUTS, INPUTS), jnp.bfloat16),
            pltpu.SemaphoreType.DMA((2,)),
            pltpu.SemaphoreType.DMA,
            pltpu.SemaphoreType.DMA((GROUPS,)),
            pltpu.SemaphoreType.DMA((2,)),
            pltpu.SemaphoreType.DMA((GROUPS,)),
            pltpu.SemaphoreType.DMA((GROUPS,)),
            pltpu.SemaphoreType.DMA((3,)),
        ],
        compiler_params=pltpu.CompilerParams(
            collective_id=0, has_side_effects=True, vmem_limit_bytes=60 * 1024 * 1024
        ),
        name="channelize",
    )(voltages, prototype, table)


def finish_kernel(
    done_hbm, last_hbm, o_hbm, received, rows, scale_col, scale_row, staged, sems, copy_sems
):
    load = pltpu.make_async_copy(last_hbm, received, sems.at[0])
    load.start()
    copies = [
        pltpu.make_async_copy(done_hbm.at[c, p], o_hbm.at[c, p], copy_sems.at[c, p])
        for c in range(3)
        for p in range(2)
    ]
    for copy in copies:
        copy.start()
    load.wait()
    correlate_channel(received, rows, scale_col, scale_row, staged)
    store = pltpu.make_async_copy(staged, o_hbm.at[3], sems.at[1])
    store.start()
    for copy in copies:
        copy.wait()
    store.wait()


def finish(done, last):
    return pl.pallas_call(
        finish_kernel,
        out_shape=jax.ShapeDtypeStruct((GROUPS, 2, INPUTS, INPUTS), jnp.bfloat16),
        in_specs=[pl.BlockSpec(memory_space=pl.ANY)] * 2,
        out_specs=pl.BlockSpec(memory_space=pl.ANY),
        scratch_shapes=[
            pltpu.VMEM((INP, TM, 2, 2, PAIRS, 128), jnp.bfloat16),
            pltpu.VMEM((INPUTS, INPUTS), jnp.bfloat16),
            pltpu.VMEM((INPUTS, 128), jnp.float32),
            pltpu.VMEM((1, INPUTS), jnp.float32),
            pltpu.VMEM((2, INPUTS, INPUTS), jnp.bfloat16),
            pltpu.SemaphoreType.DMA((2,)),
            pltpu.SemaphoreType.DMA((3, 2)),
        ],
        compiler_params=pltpu.CompilerParams(vmem_limit_bytes=60 * 1024 * 1024),
        name="finish",
    )(done, last)


def shards(voltages, prototype):
    table = jnp.asarray(dft_rows())
    return finish(*channelize(voltages, prototype, table))


def solution(mesh):
    return jax.shard_map(
        shards,
        mesh=mesh,
        in_specs=(P("inp", "tm"), P()),
        out_specs=P(("inp", "tm"), None, None, None),
        check_vma=False,
    )
```

```python
import functools
import math

import jax
import jax.numpy as jnp
import numpy as np
from jax import lax
from jax.experimental import pallas as pl
from jax.experimental.pallas import tpu as pltpu
from jax.sharding import PartitionSpec as P

TAPS = 8
HALO = TAPS - 1
AFTER = HALO // 2
BEFORE = HALO - AFTER
FRAME = 1024
INPUTS = 1024
INPUTS_DEV = 64
SPEC_DEV = 64
DEVICES = 128
GROUPS = 4
INP = 16
TM = 8
HALF = SPEC_DEV // 2
PAIRS = HALF // 2
STRIDE = PAIRS + 1
TILE = 256
MESH = pl.DeviceIdType.MESH


def dft_rows():
    channel = np.arange(DEVICES)[None, :] * GROUPS + np.arange(GROUPS)[:, None]
    sample = np.arange(FRAME)
    phase = (channel[:, :, None] * sample % FRAME) * (2.0 * math.pi / FRAME)
    table = np.stack([np.cos(phase), -np.sin(phase)], axis=2)
    return table.reshape(GROUPS, 2 * DEVICES, FRAME).astype(jnp.bfloat16)


def correlate_channel(received, rows, scale_col, scale_row, out):
    @pl.loop(0, INP)
    def _(a):
        at = pl.ds(pl.multiple_of(a * INPUTS_DEV, INPUTS_DEV), INPUTS_DEV)
        for p in range(2):
            turned = received[a, :, :, p].reshape(TM * HALF, 128).T
            for h in range(2):
                base = (2 * p + h) * TM * HALF
                rows[at, base : base + TM * HALF] = turned[h * 64 : (h + 1) * 64]

    half = INPUTS // 2

    def grams(left, right, n):
        other = rows[n * TILE : (n + 1) * TILE, :]
        dims = (((1,), (1,)), ((), ()))
        return (
            lax.dot_general(left, other, dims, preferred_element_type=jnp.float32),
            lax.dot_general(right, other, dims, preferred_element_type=jnp.float32),
        )

    def sides(m):
        left = rows[m * TILE : (m + 1) * TILE, :]
        return left, jnp.concatenate([left[:, half:], -left[:, :half]], axis=1)

    eye = lax.broadcasted_iota(jnp.int32, (TILE, TILE), 0) == lax.broadcasted_iota(
        jnp.int32, (TILE, TILE), 1
    )
    for m in range(INPUTS // TILE):
        at = slice(m * TILE, (m + 1) * TILE)
        real, imag = grams(*sides(m), m)
        diagonal = jnp.where(eye, real, 0.0)
        column = lax.rsqrt(jnp.sum(diagonal, axis=1, keepdims=True) + 1e-06)
        row = lax.rsqrt(jnp.sum(diagonal, axis=0, keepdims=True) + 1e-06)
        scale_col[at, :] = jnp.broadcast_to(column, (TILE, 128))
        scale_row[:, at] = row
        outer = column * row
        out[0, at, at] = (real * outer).astype(jnp.bfloat16)
        out[1, at, at] = (imag * outer).astype(jnp.bfloat16)
    for m in range(INPUTS // TILE - 1):
        left, right = sides(m)
        at = slice(m * TILE, (m + 1) * TILE)
        column = scale_col[at, 0:1]
        for n in range(m + 1, INPUTS // TILE):
            to = slice(n * TILE, (n + 1) * TILE)
            outer = column * scale_row[:, to]
            real, imag = grams(left, right, n)
            real = (real * outer).astype(jnp.bfloat16)
            imag = (imag * outer).astype(jnp.bfloat16)
            out[0, at, to] = real
            out[1, at, to] = imag
            out[0, to, at] = real.T
            out[1, to, at] = -imag.T


def channelize_kernel(
    v_hbm, proto_ref, table_hbm, done_hbm, last_hbm,
    v, table, filtered, turned, outbox, inbox, rows, scale_col, scale_row, staged,
    v_sems, table_sem, own_sems, halo_sems, send_sems, recv_sems, done_sems,
):
    a = lax.axis_index("inp")
    b = lax.axis_index("tm")
    me = a * TM + b
    barrier = pltpu.get_barrier_semaphore()

    def frames(first, count):
        return pl.ds(first * FRAME, count * FRAME)

    loads = [
        pltpu.make_async_copy(
            v_hbm.at[pl.ds(q * 16, 16), :],
            v.at[pl.ds(q * 16, 16), frames(BEFORE, SPEC_DEV)],
            v_sems.at[q],
        )
        for q in range(4)
    ]
    for load in loads:
        load.start()
    table_load = pltpu.make_async_copy(table_hbm, table, table_sem)
    table_load.start()

    def place(k):
        other = lax.rem(me + k * 37, DEVICES)
        return other, {"inp": lax.div(other, TM), "tm": lax.rem(other, TM)}

    @pl.loop(1, DEVICES)
    def _(k):
        _, where = place(k)
        pl.semaphore_signal(barrier, inc=1, device_id=where, device_id_type=MESH)

    def fir(chunk, q, last=False):
        at = pl.ds(pl.multiple_of(q * 16, 16), 16)
        slot = lax.rem(chunk + 6, 8) * 8
        keep = jnp.where(b < TM - 1, 1.0, 0.0) if last else None
        for nb in range(FRAME // 128):
            lanes = slice(nb * 128, (nb + 1) * 128)
            taps = [proto_ref[k : k + 1, lanes] for k in range(TAPS)]
            x = [
                v[
                    at, pl.ds(pl.multiple_of((chunk * 8 + f) * FRAME + nb * 128, 128), 128)
                ].astype(jnp.float32)
                for f in range(8 + HALO)
            ]
            for s in range(8):
                total = taps[0] * x[s]
                for k in range(1, TAPS):
                    if last and s + k == 8 + BEFORE:
                        total = total * keep
                    total = total + taps[k] * x[s + k]
                filtered[slot + s, at, lanes] = total.astype(jnp.bfloat16)

    def dft(j, half):
        block = filtered[pl.ds(half * HALF, HALF)].reshape(HALF * INPUTS_DEV, FRAME)
        out = lax.dot_general(
            table[j], block, (((1,), (1,)), ((), ())), preferred_element_type=jnp.float32
        )
        for l in range(PAIRS):
            turned[pl.ds(l, 2 * DEVICES, stride=STRIDE), :] = out[:, l * 128 : (l + 1) * 128]
        for m in range(2 * DEVICES):
            outbox[j, m // 2, half, m % 2] = turned[pl.ds(m * STRIDE, PAIRS), :].astype(
                jnp.bfloat16
            )

    def send(j, source, target):
        @pl.loop(1, DEVICES)
        def _(k):
            other, where = place(k)
            pltpu.make_async_remote_copy(
                src_ref=source(other),
                dst_ref=target,
                send_sem=send_sems.at[j],
                recv_sem=recv_sems.at[j],
                device_id=where,
                device_id_type=MESH,
            ).start()

    def halo(first, count, to, step, n):
        return pltpu.make_async_remote_copy(
            src_ref=v.at[:, frames(first, count)],
            dst_ref=v.at[:, frames(to, count)],
            send_sem=halo_sems.at[n],
            recv_sem=halo_sems.at[2 + n],
            device_id={"tm": lax.rem(b + step, TM)},
            device_id_type=MESH,
        )

    forward = halo(SPEC_DEV, BEFORE, 0, 1, 0)
    back = halo(BEFORE, AFTER, BEFORE + SPEC_DEV, TM - 1, 1)
    for load in loads:
        load.wait()
    pl.semaphore_wait(barrier, DEVICES - 1)
    back.start()

    @pl.when(b < TM - 1)
    def _():
        forward.start()

    pl.loop(0, 16)(lambda t: fir(2 + lax.div(t, 4), lax.rem(t, 4)))
    table_load.wait()

    @pl.loop(0, 2)
    def _(j):
        dft(j, 0)
        send(j, lambda other: outbox.at[j, other, 0], inbox.at[j, a, b, 0])

    pl.loop(0, 8)(lambda t: fir(6 - 5 * lax.div(t, 4), lax.rem(t, 4)))

    @pl.when(b == 0)
    def _():
        @pl.loop(0, BEFORE)
        def _(f):
            v[:, pl.ds(pl.multiple_of(f * FRAME, FRAME), FRAME)] = jnp.zeros(
                (INPUTS_DEV, FRAME), jnp.bfloat16
            )

    @pl.when(b > 0)
    def _():
        forward.wait_recv()

    pl.loop(0, 4)(lambda q: fir(0, q))
    back.wait_recv()
    pl.loop(0, 4)(lambda q: fir(7, q, True))

    @pl.loop(0, 2)
    def _(j):
        dft(j, 1)
        send(j, lambda other: outbox.at[j, other, 1], inbox.at[j, a, b, 1])

    @pl.loop(2, GROUPS)
    def _(j):
        @pl.loop(0, 2)
        def _(half):
            dft(j, half)

        @pl.when(j == 2)
        def _():
            send(2, lambda other: outbox.at[2, other], inbox.at[2, a, b])

        @pl.when(j == 3)
        def _():
            send(3, lambda other: outbox.at[3, other], last_hbm.at[a, b])

    owns = [
        pltpu.make_async_copy(
            outbox.at[j, me], inbox.at[j, a, b] if j < 3 else last_hbm.at[a, b], own_sems.at[j]
        )
        for j in range(GROUPS)
    ]
    for own in owns:
        own.start()

    back.wait_send()

    @pl.when(b < TM - 1)
    def _():
        forward.wait_send()

    def arrived(j):
        some = outbox.at[j, pl.ds(0, DEVICES - 1)]
        pltpu.make_async_copy(some, some, recv_sems.at[j]).wait()

    def written(j):
        return pltpu.make_async_copy(staged.at[lax.rem(j, 2)], done_hbm.at[j], done_sems.at[j])

    for j in range(3):
        owns[j].wait()

    @pl.loop(0, 3)
    def _(j):
        arrived(j)

        @pl.when(j == 2)
        def _():
            written(0).wait()

        correlate_channel(inbox.at[j], rows, scale_col, scale_row, staged.at[lax.rem(j, 2)])
        written(j).start()

    written(1).wait()
    written(2).wait()
    owns[3].wait()
    arrived(3)

    @pl.loop(0, GROUPS)
    def _(j):
        some = outbox.at[j, pl.ds(0, DEVICES - 1)]
        pltpu.make_async_copy(some, some, send_sems.at[j]).wait()


def channelize(voltages, prototype, table):
    piece = (INP, TM, 2, 2, PAIRS, 128)
    return pl.pallas_call(
        channelize_kernel,
        out_shape=(
            jax.ShapeDtypeStruct((3, 2, INPUTS, INPUTS), jnp.bfloat16),
            jax.ShapeDtypeStruct(piece, jnp.bfloat16),
        ),
        in_specs=[
            pl.BlockSpec(memory_space=pl.ANY),
            pl.BlockSpec(memory_space=pltpu.VMEM),
            pl.BlockSpec(memory_space=pl.ANY),
        ],
        out_specs=(pl.BlockSpec(memory_space=pl.ANY), pl.BlockSpec(memory_space=pl.ANY)),
        scratch_shapes=[
            pltpu.VMEM((INPUTS_DEV, (SPEC_DEV + HALO) * FRAME), jnp.bfloat16),
            pltpu.VMEM((GROUPS, 2 * DEVICES, FRAME), jnp.bfloat16),
            pltpu.VMEM((SPEC_DEV, INPUTS_DEV, FRAME), jnp.bfloat16),
            pltpu.VMEM((2 * DEVICES * STRIDE, 128), jnp.float32),
            pltpu.VMEM((GROUPS, DEVICES, 2, 2, PAIRS, 128), jnp.bfloat16),
            pltpu.VMEM((3, *piece), jnp.bfloat16),
            pltpu.VMEM((INPUTS, INPUTS), jnp.bfloat16),
            pltpu.VMEM((INPUTS, 128), jnp.float32),
            pltpu.VMEM((1, INPUTS), jnp.float32),
            pltpu.VMEM((2, 2, INPUTS, INPUTS), jnp.bfloat16),
            pltpu.SemaphoreType.DMA((4,)),
            pltpu.SemaphoreType.DMA,
            pltpu.SemaphoreType.DMA((GROUPS,)),
            pltpu.SemaphoreType.DMA((4,)),
            pltpu.SemaphoreType.DMA((GROUPS,)),
            pltpu.SemaphoreType.DMA((GROUPS,)),
            pltpu.SemaphoreType.DMA((3,)),
        ],
        compiler_params=pltpu.CompilerParams(
            collective_id=0, has_side_effects=True, vmem_limit_bytes=60 * 1024 * 1024
        ),
        name="channelize",
    )(voltages, prototype, table)


def finish_kernel(
    done_hbm, last_hbm, o_hbm, received, rows, scale_col, scale_row, staged, passing, sems, copy_sems
):
    load = pltpu.make_async_copy(last_hbm, received, sems.at[0])
    load.start()
    ins = [
        pltpu.make_async_copy(done_hbm.at[c, p], passing.at[c, p], copy_sems.at[0, c, p])
        for c in range(3)
        for p in range(2)
    ]
    copies = [
        pltpu.make_async_copy(passing.at[c, p], o_hbm.at[c, p], copy_sems.at[1, c, p])
        for c in range(3)
        for p in range(2)
    ]
    for copy in ins:
        copy.start()
    load.wait()
    for n, copy in enumerate(copies):
        ins[n].wait()
        copy.start()
    correlate_channel(received, rows, scale_col, scale_row, staged)
    store = pltpu.make_async_copy(staged, o_hbm.at[3], sems.at[1])
    store.start()
    for copy in copies:
        copy.wait()
    store.wait()


def finish(done, last):
    return pl.pallas_call(
        finish_kernel,
        out_shape=jax.ShapeDtypeStruct((GROUPS, 2, INPUTS, INPUTS), jnp.bfloat16),
        in_specs=[pl.BlockSpec(memory_space=pl.ANY)] * 2,
        out_specs=pl.BlockSpec(memory_space=pl.ANY),
        scratch_shapes=[
            pltpu.VMEM((INP, TM, 2, 2, PAIRS, 128), jnp.bfloat16),
            pltpu.VMEM((INPUTS, INPUTS), jnp.bfloat16),
            pltpu.VMEM((INPUTS, 128), jnp.float32),
            pltpu.VMEM((1, INPUTS), jnp.float32),
            pltpu.VMEM((2, INPUTS, INPUTS), jnp.bfloat16),
            pltpu.VMEM((3, 2, INPUTS, INPUTS), jnp.bfloat16),
            pltpu.SemaphoreType.DMA((2,)),
            pltpu.SemaphoreType.DMA((2, 3, 2)),
        ],
        compiler_params=pltpu.CompilerParams(vmem_limit_bytes=60 * 1024 * 1024),
        name="finish",
    )(done, last)


def shards(voltages, prototype):
    table = jnp.asarray(dft_rows())
    return finish(*channelize(voltages, prototype, table))


def solution(mesh):
    return jax.shard_map(
        shards,
        mesh=mesh,
        in_specs=(P("inp", "tm"), P()),
        out_specs=P(("inp", "tm"), None, None, None),
        check_vma=False,
    )
```

```python
import functools
import math

import jax
import jax.numpy as jnp
import numpy as np
from jax import lax
from jax.experimental import pallas as pl
from jax.experimental.pallas import tpu as pltpu
from jax.sharding import PartitionSpec as P

TAPS = 8
HALO = TAPS - 1
AFTER = HALO // 2
BEFORE = HALO - AFTER
FRAME = 1024
INPUTS = 1024
INPUTS_DEV = 64
SPEC_DEV = 64
DEVICES = 128
GROUPS = 4
INP = 16
TM = 8
HALF = SPEC_DEV // 2
PAIRS = HALF // 2
STRIDE = PAIRS + 1
TILE = 256
MESH = pl.DeviceIdType.MESH


def dft_rows():
    channel = np.arange(DEVICES)[None, :] * GROUPS + np.arange(GROUPS)[:, None]
    sample = np.arange(FRAME)
    phase = (channel[:, :, None] * sample % FRAME) * (2.0 * math.pi / FRAME)
    table = np.stack([np.cos(phase), -np.sin(phase)], axis=2)
    return table.reshape(GROUPS, 2 * DEVICES, FRAME).astype(jnp.bfloat16)


def correlate_channel(received, rows, scale_col, scale_row, out):
    @pl.loop(0, INP)
    def _(a):
        at = pl.ds(pl.multiple_of(a * INPUTS_DEV, INPUTS_DEV), INPUTS_DEV)
        for p in range(2):
            turned = received[a, :, :, p].reshape(TM * HALF, 128).T
            for h in range(2):
                base = (2 * p + h) * TM * HALF
                rows[at, base : base + TM * HALF] = turned[h * 64 : (h + 1) * 64]

    half = INPUTS // 2

    def grams(left, right, n):
        other = rows[n * TILE : (n + 1) * TILE, :]
        dims = (((1,), (1,)), ((), ()))
        return (
            lax.dot_general(left, other, dims, preferred_element_type=jnp.float32),
            lax.dot_general(right, other, dims, preferred_element_type=jnp.float32),
        )

    def sides(m):
        left = rows[m * TILE : (m + 1) * TILE, :]
        return left, jnp.concatenate([left[:, half:], -left[:, :half]], axis=1)

    eye = lax.broadcasted_iota(jnp.int32, (TILE, TILE), 0) == lax.broadcasted_iota(
        jnp.int32, (TILE, TILE), 1
    )
    for m in range(INPUTS // TILE):
        at = slice(m * TILE, (m + 1) * TILE)
        real, imag = grams(*sides(m), m)
        diagonal = jnp.where(eye, real, 0.0)
        column = lax.rsqrt(jnp.sum(diagonal, axis=1, keepdims=True) + 1e-06)
        row = lax.rsqrt(jnp.sum(diagonal, axis=0, keepdims=True) + 1e-06)
        scale_col[at, :] = jnp.broadcast_to(column, (TILE, 128))
        scale_row[:, at] = row
        outer = column * row
        out[0, at, at] = (real * outer).astype(jnp.bfloat16)
        out[1, at, at] = (imag * outer).astype(jnp.bfloat16)
    for m in range(INPUTS // TILE - 1):
        left, right = sides(m)
        at = slice(m * TILE, (m + 1) * TILE)
        column = scale_col[at, 0:1]
        for n in range(m + 1, INPUTS // TILE):
            to = slice(n * TILE, (n + 1) * TILE)
            outer = column * scale_row[:, to]
            real, imag = grams(left, right, n)
            real = (real * outer).astype(jnp.bfloat16)
            imag = (imag * outer).astype(jnp.bfloat16)
            out[0, at, to] = real
            out[1, at, to] = imag
            out[0, to, at] = real.T
            out[1, to, at] = -imag.T


def channelize_kernel(
    v_hbm, proto_ref, table_hbm, done, last,
    v, table, filtered, turned, outbox, inbox, rows, scale_col, scale_row,
    v_sems, table_sem, own_sems, halo_sems, send_sems, recv_sems,
):
    a = lax.axis_index("inp")
    b = lax.axis_index("tm")
    me = a * TM + b
    barrier = pltpu.get_barrier_semaphore()

    def frames(first, count):
        return pl.ds(first * FRAME, count * FRAME)

    loads = [
        pltpu.make_async_copy(
            v_hbm.at[pl.ds(q * 16, 16), :],
            v.at[pl.ds(q * 16, 16), frames(BEFORE, SPEC_DEV)],
            v_sems.at[q],
        )
        for q in range(4)
    ]
    for load in loads:
        load.start()
    table_load = pltpu.make_async_copy(table_hbm, table, table_sem)
    table_load.start()

    def place(k):
        other = lax.rem(me + k * 37, DEVICES)
        return other, {"inp": lax.div(other, TM), "tm": lax.rem(other, TM)}

    @pl.loop(1, DEVICES)
    def _(k):
        _, where = place(k)
        pl.semaphore_signal(barrier, inc=1, device_id=where, device_id_type=MESH)

    def fir(chunk, q, last=False):
        at = pl.ds(pl.multiple_of(q * 16, 16), 16)
        slot = lax.rem(chunk + 6, 8) * 8
        keep = jnp.where(b < TM - 1, 1.0, 0.0) if last else None
        for nb in range(FRAME // 128):
            lanes = slice(nb * 128, (nb + 1) * 128)
            taps = [proto_ref[k : k + 1, lanes] for k in range(TAPS)]
            x = [
                v[
                    at, pl.ds(pl.multiple_of((chunk * 8 + f) * FRAME + nb * 128, 128), 128)
                ].astype(jnp.float32)
                for f in range(8 + HALO)
            ]
            for s in range(8):
                total = taps[0] * x[s]
                for k in range(1, TAPS):
                    if last and s + k == 8 + BEFORE:
                        total = total * keep
                    total = total + taps[k] * x[s + k]
                filtered[slot + s, at, lanes] = total.astype(jnp.bfloat16)

    def dft(j, half):
        block = filtered[pl.ds(half * HALF, HALF)].reshape(HALF * INPUTS_DEV, FRAME)
        out = lax.dot_general(
            table[j], block, (((1,), (1,)), ((), ())), preferred_element_type=jnp.float32
        )
        for l in range(PAIRS):
            turned[pl.ds(l, 2 * DEVICES, stride=STRIDE), :] = out[:, l * 128 : (l + 1) * 128]
        for m in range(2 * DEVICES):
            outbox[j, m // 2, half, m % 2] = turned[pl.ds(m * STRIDE, PAIRS), :].astype(
                jnp.bfloat16
            )

    def send(j, source, target):
        @pl.loop(1, DEVICES)
        def _(k):
            other, where = place(k)
            pltpu.make_async_remote_copy(
                src_ref=source(other),
                dst_ref=target,
                send_sem=send_sems.at[j],
                recv_sem=recv_sems.at[j],
                device_id=where,
                device_id_type=MESH,
            ).start()

    def halo(first, count, to, step, n):
        return pltpu.make_async_remote_copy(
            src_ref=v.at[:, frames(first, count)],
            dst_ref=v.at[:, frames(to, count)],
            send_sem=halo_sems.at[n],
            recv_sem=halo_sems.at[2 + n],
            device_id={"tm": lax.rem(b + step, TM)},
            device_id_type=MESH,
        )

    forward = halo(SPEC_DEV, BEFORE, 0, 1, 0)
    back = halo(BEFORE, AFTER, BEFORE + SPEC_DEV, TM - 1, 1)
    for load in loads:
        load.wait()
    pl.semaphore_wait(barrier, DEVICES - 1)
    back.start()

    @pl.when(b < TM - 1)
    def _():
        forward.start()

    pl.loop(0, 16)(lambda t: fir(2 + lax.div(t, 4), lax.rem(t, 4)))
    table_load.wait()

    @pl.loop(0, 2)
    def _(j):
        dft(j, 0)
        send(j, lambda other: outbox.at[j, other, 0], inbox.at[j, a, b, 0])

    pl.loop(0, 8)(lambda t: fir(6 - 5 * lax.div(t, 4), lax.rem(t, 4)))

    @pl.when(b == 0)
    def _():
        @pl.loop(0, BEFORE)
        def _(f):
            v[:, pl.ds(pl.multiple_of(f * FRAME, FRAME), FRAME)] = jnp.zeros(
                (INPUTS_DEV, FRAME), jnp.bfloat16
            )

    @pl.when(b > 0)
    def _():
        forward.wait_recv()

    pl.loop(0, 4)(lambda q: fir(0, q))
    back.wait_recv()
    pl.loop(0, 4)(lambda q: fir(7, q, True))

    @pl.loop(0, 2)
    def _(j):
        dft(j, 1)
        send(j, lambda other: outbox.at[j, other, 1], inbox.at[j, a, b, 1])

    @pl.loop(2, GROUPS)
    def _(j):
        @pl.loop(0, 2)
        def _(half):
            dft(j, half)

        @pl.when(j == 2)
        def _():
            send(2, lambda other: outbox.at[2, other], inbox.at[2, a, b])

        @pl.when(j == 3)
        def _():
            send(3, lambda other: outbox.at[3, other], last.at[a, b])

    owns = [
        pltpu.make_async_copy(
            outbox.at[j, me], inbox.at[j, a, b] if j < 3 else last.at[a, b], own_sems.at[j]
        )
        for j in range(GROUPS)
    ]
    for own in owns:
        own.start()

    back.wait_send()

    @pl.when(b < TM - 1)
    def _():
        forward.wait_send()

    def arrived(j):
        some = outbox.at[j, pl.ds(0, DEVICES - 1)]
        pltpu.make_async_copy(some, some, recv_sems.at[j]).wait()

    for j in range(3):
        owns[j].wait()

    @pl.loop(0, 3)
    def _(j):
        arrived(j)

        correlate_channel(inbox.at[j], rows, scale_col, scale_row, done.at[j])

    owns[3].wait()
    arrived(3)

    @pl.loop(0, GROUPS)
    def _(j):
        some = outbox.at[j, pl.ds(0, DEVICES - 1)]
        pltpu.make_async_copy(some, some, send_sems.at[j]).wait()


def channelize(voltages, prototype, table):
    piece = (INP, TM, 2, 2, PAIRS, 128)
    return pl.pallas_call(
        channelize_kernel,
        out_shape=(
            pltpu.VMEM((3, 2, INPUTS, INPUTS), jnp.bfloat16),
            pltpu.VMEM(piece, jnp.bfloat16),
        ),
        in_specs=[
            pl.BlockSpec(memory_space=pl.ANY),
            pl.BlockSpec(memory_space=pltpu.VMEM),
            pl.BlockSpec(memory_space=pl.ANY),
        ],
        out_specs=(pl.BlockSpec(memory_space=pltpu.VMEM), pl.BlockSpec(memory_space=pltpu.VMEM)),
        scratch_shapes=[
            pltpu.VMEM((INPUTS_DEV, (SPEC_DEV + HALO) * FRAME), jnp.bfloat16),
            pltpu.VMEM((GROUPS, 2 * DEVICES, FRAME), jnp.bfloat16),
            pltpu.VMEM((SPEC_DEV, INPUTS_DEV, FRAME), jnp.bfloat16),
            pltpu.VMEM((2 * DEVICES * STRIDE, 128), jnp.float32),
            pltpu.VMEM((GROUPS, DEVICES, 2, 2, PAIRS, 128), jnp.bfloat16),
            pltpu.VMEM((3, *piece), jnp.bfloat16),
            pltpu.VMEM((INPUTS, INPUTS), jnp.bfloat16),
            pltpu.VMEM((INPUTS, 128), jnp.float32),
            pltpu.VMEM((1, INPUTS), jnp.float32),
            pltpu.SemaphoreType.DMA((4,)),
            pltpu.SemaphoreType.DMA,
            pltpu.SemaphoreType.DMA((GROUPS,)),
            pltpu.SemaphoreType.DMA((4,)),
            pltpu.SemaphoreType.DMA((GROUPS,)),
            pltpu.SemaphoreType.DMA((GROUPS,)),
        ],
        compiler_params=pltpu.CompilerParams(
            collective_id=0, has_side_effects=True, vmem_limit_bytes=42 * 1024 * 1024
        ),
        name="channelize",
    )(voltages, prototype, table)


def finish_kernel(done, last, o_hbm, rows, scale_col, scale_row, staged, sems):
    copies = [pltpu.make_async_copy(done.at[c], o_hbm.at[c], sems.at[c]) for c in range(3)]
    for copy in copies:
        copy.start()
    correlate_channel(last, rows, scale_col, scale_row, staged)
    copies.append(pltpu.make_async_copy(staged, o_hbm.at[3], sems.at[3]))
    copies[3].start()
    for copy in copies:
        copy.wait()


def finish(done, last):
    return pl.pallas_call(
        finish_kernel,
        out_shape=jax.ShapeDtypeStruct((GROUPS, 2, INPUTS, INPUTS), jnp.bfloat16),
        in_specs=[pl.BlockSpec(memory_space=pltpu.VMEM)] * 2,
        out_specs=pl.BlockSpec(memory_space=pl.ANY),
        scratch_shapes=[
            pltpu.VMEM((INPUTS, INPUTS), jnp.bfloat16),
            pltpu.VMEM((INPUTS, 128), jnp.float32),
            pltpu.VMEM((1, INPUTS), jnp.float32),
            pltpu.VMEM((2, INPUTS, INPUTS), jnp.bfloat16),
            pltpu.SemaphoreType.DMA((GROUPS,)),
        ],
        compiler_params=pltpu.CompilerParams(vmem_limit_bytes=20 * 1024 * 1024),
        name="finish",
    )(done, last)


def shards(voltages, prototype):
    table = jnp.asarray(dft_rows())
    return finish(*channelize(voltages, prototype, table))


def solution(mesh):
    return jax.shard_map(
        shards,
        mesh=mesh,
        in_specs=(P("inp", "tm"), P()),
        out_specs=P(("inp", "tm"), None, None, None),
        check_vma=False,
    )
```

```python
import functools
import math

import jax
import jax.numpy as jnp
import numpy as np
from jax import lax
from jax.experimental import pallas as pl
from jax.experimental.pallas import tpu as pltpu
from jax.sharding import PartitionSpec as P

TAPS = 8
HALO = TAPS - 1
AFTER = HALO // 2
BEFORE = HALO - AFTER
FRAME = 1024
INPUTS = 1024
INPUTS_DEV = 64
SPEC_DEV = 64
DEVICES = 128
GROUPS = 4
INP = 16
TM = 8
QUARTERS = 4
QUARTER = SPEC_DEV // QUARTERS
PAIRS = QUARTER // 2
STRIDE = PAIRS + 1
TILE = 256
MESH = pl.DeviceIdType.MESH


def dft_rows():
    channel = np.arange(DEVICES)[None, :] * GROUPS + np.arange(GROUPS)[:, None]
    sample = np.arange(FRAME)
    phase = (channel[:, :, None] * sample % FRAME) * (2.0 * math.pi / FRAME)
    table = np.stack([np.cos(phase), -np.sin(phase)], axis=2)
    return table.reshape(GROUPS, 2 * DEVICES, FRAME).astype(jnp.bfloat16)


def correlate_channel(received, rows, swapped, scale_col, scale_row, out, finished=None):
    half = INPUTS // 2

    @pl.loop(0, INP)
    def _(a):
        at = pl.ds(pl.multiple_of(a * INPUTS_DEV, INPUTS_DEV), INPUTS_DEV)
        turned = received[a].reshape(half, 128).T
        for h in range(2):
            rows[at, h * half : (h + 1) * half] = turned[h * 64 : (h + 1) * 64]

    def grams(m, n):
        other = rows[n * TILE : (n + 1) * TILE, :]
        dims = (((1,), (1,)), ((), ()))
        return [
            lax.dot_general(
                ref[m * TILE : (m + 1) * TILE, :], other, dims, preferred_element_type=jnp.float32
            )
            for ref in (rows, swapped)
        ]

    first = lax.rem(lax.broadcasted_iota(jnp.int32, (TILE, 128), 1), 2 * PAIRS) < PAIRS
    eye = lax.broadcasted_iota(jnp.int32, (TILE, TILE), 0) == lax.broadcasted_iota(
        jnp.int32, (TILE, TILE), 1
    )
    for m in range(INPUTS // TILE):
        at = slice(m * TILE, (m + 1) * TILE)
        for n in range(INPUTS // 128):
            to = slice(n * 128, (n + 1) * 128)
            some = rows[at, to]
            ahead = pltpu.roll(some, 128 - PAIRS, 1)
            swapped[at, to] = jnp.where(first, ahead, -pltpu.roll(some, PAIRS, 1))
        real, imag = grams(m, m)
        diagonal = jnp.where(eye, real, 0.0)
        column = lax.rsqrt(jnp.sum(diagonal, axis=1, keepdims=True) + 1e-06)
        row = lax.rsqrt(jnp.sum(diagonal, axis=0, keepdims=True) + 1e-06)
        scale_col[at, :] = jnp.broadcast_to(column, (TILE, 128))
        scale_row[:, at] = row
        outer = column * row
        out[0, at, at] = (real * outer).astype(jnp.bfloat16)
        out[1, at, at] = (imag * outer).astype(jnp.bfloat16)
    for m in range(INPUTS // TILE - 1):
        at = slice(m * TILE, (m + 1) * TILE)
        column = scale_col[at, 0:1]
        for n in range(m + 1, INPUTS // TILE):
            to = slice(n * TILE, (n + 1) * TILE)
            outer = column * scale_row[:, to]
            real, imag = grams(m, n)
            real = (real * outer).astype(jnp.bfloat16)
            imag = (imag * outer).astype(jnp.bfloat16)
            out[0, at, to] = real
            out[1, at, to] = imag
            out[0, to, at] = real.T
            out[1, to, at] = -imag.T
        if finished is not None:
            finished(m)


def channelize_kernel(
    v_hbm, proto_ref, table_hbm, done, last,
    v, table, filtered, turned, outbox, inbox, rows, swapped, scale_col, scale_row,
    v_sems, table_sem, own_sems, halo_sems, send_sems, recv_sems,
):
    a = lax.axis_index("inp")
    b = lax.axis_index("tm")
    me = a * TM + b
    barrier = pltpu.get_barrier_semaphore()

    def frames(first, count):
        return pl.ds(first * FRAME, count * FRAME)

    loads = [
        pltpu.make_async_copy(
            v_hbm.at[:, frames(first, count)], v.at[:, frames(BEFORE + first, count)], v_sems.at[n]
        )
        for n, (first, count) in enumerate(((12, 23), (35, 29), (0, 12)))
    ]
    for load in loads:
        load.start()
    table_load = pltpu.make_async_copy(table_hbm, table, table_sem)
    table_load.start()

    def place(k):
        other = lax.rem(me + k * 37, DEVICES)
        return other, {"inp": lax.div(other, TM), "tm": lax.rem(other, TM)}

    @pl.loop(1, DEVICES)
    def _(k):
        _, where = place(k)
        pl.semaphore_signal(barrier, inc=1, device_id=where, device_id_type=MESH)

    def fir(chunk, q, last=False):
        at = pl.ds(pl.multiple_of(q * 16, 16), 16)
        slot = lax.rem(chunk + 6, 8) * 8
        keep = jnp.where(b < TM - 1, 1.0, 0.0) if last else None
        for nb in range(FRAME // 128):
            lanes = slice(nb * 128, (nb + 1) * 128)
            taps = [proto_ref[k : k + 1, lanes] for k in range(TAPS)]
            x = [
                v[
                    at, pl.ds(pl.multiple_of((chunk * 8 + f) * FRAME + nb * 128, 128), 128)
                ].astype(jnp.float32)
                for f in range(8 + HALO)
            ]
            for s in range(8):
                total = taps[0] * x[s]
                for k in range(1, TAPS):
                    if last and s + k == 8 + BEFORE:
                        total = total * keep
                    total = total + taps[k] * x[s + k]
                filtered[slot + s, at, lanes] = total.astype(jnp.bfloat16)

    def dft(j, quarter):
        block = filtered[pl.ds(quarter * QUARTER, QUARTER)].reshape(QUARTER * INPUTS_DEV, FRAME)
        out = lax.dot_general(
            table[j], block, (((1,), (1,)), ((), ())), preferred_element_type=jnp.float32
        )
        for l in range(PAIRS):
            turned[pl.ds(l, 2 * DEVICES, stride=STRIDE), :] = out[:, l * 128 : (l + 1) * 128]
        for d in range(DEVICES):
            parts = [turned[pl.ds((2 * d + p) * STRIDE, PAIRS), :] for p in range(2)]
            outbox[j, d, quarter] = jnp.concatenate(parts, axis=0).astype(jnp.bfloat16)

    def send(j, source, target):
        @pl.loop(1, DEVICES)
        def _(k):
            other, where = place(k)
            pltpu.make_async_remote_copy(
                src_ref=source(other),
                dst_ref=target,
                send_sem=send_sems.at[j],
                recv_sem=recv_sems.at[j],
                device_id=where,
                device_id_type=MESH,
            ).start()

    def halo(first, count, to, step, n):
        return pltpu.make_async_remote_copy(
            src_ref=v.at[:, frames(first, count)],
            dst_ref=v.at[:, frames(to, count)],
            send_sem=halo_sems.at[n],
            recv_sem=halo_sems.at[2 + n],
            device_id={"tm": lax.rem(b + step, TM)},
            device_id_type=MESH,
        )

    forward = halo(SPEC_DEV, BEFORE, 0, 1, 0)
    back = halo(BEFORE, AFTER, BEFORE + SPEC_DEV, TM - 1, 1)
    loads[0].wait()
    pl.loop(0, 4)(lambda q: fir(2, q))
    loads[1].wait()
    loads[2].wait()
    pl.semaphore_wait(barrier, DEVICES - 1)
    back.start()

    @pl.when(b < TM - 1)
    def _():
        forward.start()

    pl.loop(0, 4)(lambda q: fir(3, q))
    table_load.wait()

    @pl.loop(0, 2)
    def _(quarter):
        @pl.when(quarter == 1)
        def _():
            pl.loop(0, 8)(lambda t: fir(4 + lax.div(t, 4), lax.rem(t, 4)))

        dft(0, quarter)
        send(0, lambda other: outbox.at[0, other, quarter], inbox.at[0, a, b, quarter])

    low = pl.ds(0, 2)
    high = pl.ds(2, 2)
    pl.loop(0, 2)(lambda quarter: dft(1, quarter))
    send(1, lambda other: outbox.at[1, other, low], inbox.at[1, a, b, low])

    pl.loop(0, 8)(lambda t: fir(6 - 5 * lax.div(t, 4), lax.rem(t, 4)))

    @pl.when(b == 0)
    def _():
        @pl.loop(0, BEFORE)
        def _(f):
            v[:, pl.ds(pl.multiple_of(f * FRAME, FRAME), FRAME)] = jnp.zeros(
                (INPUTS_DEV, FRAME), jnp.bfloat16
            )

    @pl.when(b > 0)
    def _():
        forward.wait_recv()

    pl.loop(0, 4)(lambda q: fir(0, q))
    back.wait_recv()
    pl.loop(0, 4)(lambda q: fir(7, q, True))

    @pl.loop(0, 2)
    def _(j):
        pl.loop(2, 4)(lambda quarter: dft(j, quarter))
        send(j, lambda other: outbox.at[j, other, high], inbox.at[j, a, b, high])

    @pl.loop(2, GROUPS)
    def _(j):
        pl.loop(0, QUARTERS)(lambda quarter: dft(j, quarter))

        @pl.when(j == 2)
        def _():
            send(2, lambda other: outbox.at[2, other], inbox.at[2, a, b])

        @pl.when(j == 3)
        def _():
            send(3, lambda other: outbox.at[3, other], last.at[a, b])

    owns = [
        pltpu.make_async_copy(
            outbox.at[j, me], inbox.at[j, a, b] if j < 3 else last.at[a, b], own_sems.at[j]
        )
        for j in range(GROUPS)
    ]
    for own in owns:
        own.start()

    back.wait_send()

    @pl.when(b < TM - 1)
    def _():
        forward.wait_send()

    def arrived(j):
        some = outbox.at[j, pl.ds(0, DEVICES - 1)]
        pltpu.make_async_copy(some, some, recv_sems.at[j]).wait()

    for j in range(3):
        owns[j].wait()

    @pl.loop(0, 3)
    def _(j):
        arrived(j)

        correlate_channel(inbox.at[j], rows, swapped, scale_col, scale_row, done.at[j])

    owns[3].wait()
    arrived(3)

    @pl.loop(0, GROUPS)
    def _(j):
        some = outbox.at[j, pl.ds(0, DEVICES - 1)]
        pltpu.make_async_copy(some, some, send_sems.at[j]).wait()


def channelize(voltages, prototype, table):
    piece = (INP, TM, QUARTERS, 2 * PAIRS, 128)
    return pl.pallas_call(
        channelize_kernel,
        out_shape=(
            pltpu.VMEM((3, 2, INPUTS, INPUTS), jnp.bfloat16),
            pltpu.VMEM(piece, jnp.bfloat16),
        ),
        in_specs=[
            pl.BlockSpec(memory_space=pl.ANY),
            pl.BlockSpec(memory_space=pltpu.VMEM),
            pl.BlockSpec(memory_space=pl.ANY),
        ],
        out_specs=(pl.BlockSpec(memory_space=pltpu.VMEM), pl.BlockSpec(memory_space=pltpu.VMEM)),
        scratch_shapes=[
            pltpu.VMEM((INPUTS_DEV, (SPEC_DEV + HALO) * FRAME), jnp.bfloat16),
            pltpu.VMEM((GROUPS, 2 * DEVICES, FRAME), jnp.bfloat16),
            pltpu.VMEM((SPEC_DEV, INPUTS_DEV, FRAME), jnp.bfloat16),
            pltpu.VMEM((2 * DEVICES * STRIDE, 128), jnp.float32),
            pltpu.VMEM((GROUPS, DEVICES, QUARTERS, 2 * PAIRS, 128), jnp.bfloat16),
            pltpu.VMEM((3, *piece), jnp.bfloat16),
            pltpu.VMEM((INPUTS, INPUTS), jnp.bfloat16),
            pltpu.VMEM((INPUTS, INPUTS), jnp.bfloat16),
            pltpu.VMEM((INPUTS, 128), jnp.float32),
            pltpu.VMEM((1, INPUTS), jnp.float32),
            pltpu.SemaphoreType.DMA((3,)),
            pltpu.SemaphoreType.DMA,
            pltpu.SemaphoreType.DMA((GROUPS,)),
            pltpu.SemaphoreType.DMA((4,)),
            pltpu.SemaphoreType.DMA((GROUPS,)),
            pltpu.SemaphoreType.DMA((GROUPS,)),
        ],
        compiler_params=pltpu.CompilerParams(
            collective_id=0, has_side_effects=True, vmem_limit_bytes=43 * 1024 * 1024
        ),
        name="channelize",
    )(voltages, prototype, table)


def finish_kernel(done, last, o_hbm, rows, swapped, scale_col, scale_row, staged, sems):
    copies = [pltpu.make_async_copy(done.at[c], o_hbm.at[c], sems.at[c]) for c in range(3)]
    for copy in copies:
        copy.start()

    def finished(m):
        at = pl.ds(m * TILE, TILE if m < 2 else 2 * TILE)
        copies.append(
            pltpu.make_async_copy(staged.at[:, at], o_hbm.at[3, :, at], sems.at[3 + m])
        )
        copies[-1].start()

    correlate_channel(last, rows, swapped, scale_col, scale_row, staged, finished)
    for copy in copies:
        copy.wait()


def finish(done, last):
    return pl.pallas_call(
        finish_kernel,
        out_shape=jax.ShapeDtypeStruct((GROUPS, 2, INPUTS, INPUTS), jnp.bfloat16),
        in_specs=[pl.BlockSpec(memory_space=pltpu.VMEM)] * 2,
        out_specs=pl.BlockSpec(memory_space=pl.ANY),
        scratch_shapes=[
            pltpu.VMEM((INPUTS, INPUTS), jnp.bfloat16),
            pltpu.VMEM((INPUTS, INPUTS), jnp.bfloat16),
            pltpu.VMEM((INPUTS, 128), jnp.float32),
            pltpu.VMEM((1, INPUTS), jnp.float32),
            pltpu.VMEM((2, INPUTS, INPUTS), jnp.bfloat16),
            pltpu.SemaphoreType.DMA((6,)),
        ],
        compiler_params=pltpu.CompilerParams(vmem_limit_bytes=20 * 1024 * 1024),
        name="finish",
    )(done, last)


def shards(voltages, prototype):
    table = jnp.asarray(dft_rows())
    return finish(*channelize(voltages, prototype, table))


def solution(mesh):
    return jax.shard_map(
        shards,
        mesh=mesh,
        in_specs=(P("inp", "tm"), P()),
        out_specs=P(("inp", "tm"), None, None, None),
        check_vma=False,
    )
```

```python
import functools
import math

import jax
import jax.numpy as jnp
import numpy as np
from jax import lax
from jax.experimental import pallas as pl
from jax.experimental.pallas import tpu as pltpu
from jax.sharding import PartitionSpec as P

TAPS = 8
HALO = TAPS - 1
AFTER = HALO // 2
BEFORE = HALO - AFTER
FRAME = 1024
INPUTS = 1024
INPUTS_DEV = 64
SPEC_DEV = 64
DEVICES = 128
GROUPS = 4
INP = 16
TM = 8
QUARTERS = 4
QUARTER = SPEC_DEV // QUARTERS
PAIRS = QUARTER // 2
STRIDE = PAIRS + 1
TILE = 256
MESH = pl.DeviceIdType.MESH


def dft_rows():
    channel = np.arange(DEVICES)[None, :] * GROUPS + np.arange(GROUPS)[:, None]
    sample = np.arange(FRAME)
    phase = (channel[:, :, None] * sample % FRAME) * (2.0 * math.pi / FRAME)
    table = np.stack([np.cos(phase), -np.sin(phase)], axis=2)
    return table.reshape(GROUPS, 2 * DEVICES, FRAME).astype(jnp.bfloat16)


def correlate_channel(received, rows, swapped, scale_col, scale_row, out, finished=None):
    half = INPUTS // 2

    @pl.loop(0, INP)
    def _(a):
        at = pl.ds(pl.multiple_of(a * INPUTS_DEV, INPUTS_DEV), INPUTS_DEV)
        turned = received[a].reshape(half, 128).T
        for h in range(2):
            rows[at, h * half : (h + 1) * half] = turned[h * 64 : (h + 1) * 64]

    def grams(m, n):
        other = rows[n * TILE : (n + 1) * TILE, :]
        dims = (((1,), (1,)), ((), ()))
        return [
            lax.dot_general(
                ref[m * TILE : (m + 1) * TILE, :], other, dims, preferred_element_type=jnp.float32
            )
            for ref in (rows, swapped)
        ]

    first = lax.rem(lax.broadcasted_iota(jnp.int32, (TILE, 128), 1), 2 * PAIRS) < PAIRS
    eye = lax.broadcasted_iota(jnp.int32, (TILE, TILE), 0) == lax.broadcasted_iota(
        jnp.int32, (TILE, TILE), 1
    )
    for m in range(INPUTS // TILE):
        at = slice(m * TILE, (m + 1) * TILE)
        for n in range(INPUTS // 128):
            to = slice(n * 128, (n + 1) * 128)
            some = rows[at, to]
            ahead = pltpu.roll(some, 128 - PAIRS, 1)
            swapped[at, to] = jnp.where(first, ahead, -pltpu.roll(some, PAIRS, 1))
        real, imag = grams(m, m)
        diagonal = jnp.where(eye, real, 0.0)
        column = lax.rsqrt(jnp.sum(diagonal, axis=1, keepdims=True) + 1e-06)
        row = lax.rsqrt(jnp.sum(diagonal, axis=0, keepdims=True) + 1e-06)
        scale_col[at, :] = jnp.broadcast_to(column, (TILE, 128))
        scale_row[:, at] = row
        outer = column * row
        out[0, at, at] = (real * outer).astype(jnp.bfloat16)
        out[1, at, at] = (imag * outer).astype(jnp.bfloat16)
    for m in range(INPUTS // TILE - 1):
        at = slice(m * TILE, (m + 1) * TILE)
        column = scale_col[at, 0:1]
        for n in range(m + 1, INPUTS // TILE):
            to = slice(n * TILE, (n + 1) * TILE)
            outer = column * scale_row[:, to]
            real, imag = grams(m, n)
            real = (real * outer).astype(jnp.bfloat16)
            imag = (imag * outer).astype(jnp.bfloat16)
            out[0, at, to] = real
            out[1, at, to] = imag
            out[0, to, at] = real.T
            out[1, to, at] = -imag.T
        if finished is not None:
            finished(m)


def channelize_kernel(
    v_hbm, proto_ref, table_hbm, done, last,
    v, table, filtered, turned, outbox, inbox, rows, swapped, scale_col, scale_row,
    v_sems, table_sem, own_sems, halo_sems, send_sems, recv_sems, row_sem,
):
    a = lax.axis_index("inp")
    b = lax.axis_index("tm")
    me = a * TM + b
    barrier = pltpu.get_barrier_semaphore()

    def frames(first, count):
        return pl.ds(pl.multiple_of(first * FRAME, FRAME), count * FRAME)

    loads = [
        pltpu.make_async_copy(
            v_hbm.at[:, frames(first, count)], v.at[:, frames(BEFORE + first, count)], v_sems.at[n]
        )
        for n, (first, count) in enumerate(((12, 24), (36, 28), (0, 12)))
    ]
    for load in loads:
        load.start()
    table_load = pltpu.make_async_copy(table_hbm, table, table_sem)
    table_load.start()

    def place(k):
        other = lax.rem(me + k * 37, DEVICES)
        return other, {"inp": lax.div(other, TM), "tm": lax.rem(other, TM)}

    @pl.loop(1, INP)
    def _(k):
        pl.semaphore_signal(
            barrier, inc=1, device_id={"inp": lax.rem(a + k, INP)}, device_id_type=MESH
        )

    def signal_row(semaphore):
        @pl.loop(1, TM)
        def _(k):
            pl.semaphore_signal(
                semaphore, inc=1, device_id={"tm": lax.rem(b + k, TM)}, device_id_type=MESH
            )

    signal_row(barrier)

    def fir(chunk, q, last=False):
        at = pl.ds(pl.multiple_of(q * 16, 16), 16)
        slot = lax.rem(chunk + 6, 8) * 8
        keep = jnp.where(b < TM - 1, 1.0, 0.0) if last else None
        for nb in range(FRAME // 128):
            lanes = slice(nb * 128, (nb + 1) * 128)
            taps = [proto_ref[k : k + 1, lanes] for k in range(TAPS)]
            x = [
                v[
                    at, pl.ds(pl.multiple_of((chunk * 8 + f) * FRAME + nb * 128, 128), 128)
                ].astype(jnp.float32)
                for f in range(8 + HALO)
            ]
            for s in range(8):
                total = taps[0] * x[s]
                for k in range(1, TAPS):
                    if last and s + k == 8 + BEFORE:
                        total = total * keep
                    total = total + taps[k] * x[s + k]
                filtered[slot + s, at, lanes] = total.astype(jnp.bfloat16)

    def dft(j, quarter):
        block = filtered[pl.ds(quarter * QUARTER, QUARTER)].reshape(QUARTER * INPUTS_DEV, FRAME)
        out = lax.dot_general(
            table[j], block, (((1,), (1,)), ((), ())), preferred_element_type=jnp.float32
        )
        for l in range(PAIRS):
            turned[pl.ds(l, 2 * DEVICES, stride=STRIDE), :] = out[:, l * 128 : (l + 1) * 128]
        for d in range(DEVICES):
            parts = [turned[pl.ds((2 * d + p) * STRIDE, PAIRS), :] for p in range(2)]
            outbox[j, d, quarter] = jnp.concatenate(parts, axis=0).astype(jnp.bfloat16)

    def send(j, source, target):
        @pl.loop(1, DEVICES)
        def _(k):
            other, where = place(k)
            pltpu.make_async_remote_copy(
                src_ref=source(other),
                dst_ref=target,
                send_sem=send_sems.at[j],
                recv_sem=recv_sems.at[j],
                device_id=where,
                device_id_type=MESH,
            ).start()

    def halo(first, count, to, step, n):
        return pltpu.make_async_remote_copy(
            src_ref=v.at[:, frames(first, count)],
            dst_ref=v.at[:, frames(to, count)],
            send_sem=halo_sems.at[n],
            recv_sem=halo_sems.at[2 + n],
            device_id={"tm": lax.rem(b + step, TM)},
            device_id_type=MESH,
        )

    forward = halo(SPEC_DEV, BEFORE, 0, 1, 0)
    back = halo(BEFORE, AFTER, BEFORE + SPEC_DEV, TM - 1, 1)
    loads[0].wait()
    pl.loop(0, 4)(lambda q: fir(2, q))
    loads[1].wait()
    loads[2].wait()
    pl.semaphore_wait(barrier, INP + TM - 2)
    back.start()

    @pl.when(b < TM - 1)
    def _():
        forward.start()

    signal_row(row_sem)

    pl.loop(0, 4)(lambda q: fir(3, q))
    table_load.wait()
    pl.semaphore_wait(row_sem, TM - 1)

    @pl.loop(0, 2)
    def _(quarter):
        @pl.when(quarter == 1)
        def _():
            pl.loop(0, 8)(lambda t: fir(4 + lax.div(t, 4), lax.rem(t, 4)))

        dft(0, quarter)
        send(0, lambda other: outbox.at[0, other, quarter], inbox.at[0, a, b, quarter])

    low = pl.ds(0, 2)
    high = pl.ds(2, 2)
    pl.loop(0, 2)(lambda quarter: dft(1, quarter))
    send(1, lambda other: outbox.at[1, other, low], inbox.at[1, a, b, low])

    pl.loop(0, 8)(lambda t: fir(6 - 5 * lax.div(t, 4), lax.rem(t, 4)))

    @pl.when(b == 0)
    def _():
        @pl.loop(0, BEFORE)
        def _(f):
            v[:, pl.ds(pl.multiple_of(f * FRAME, FRAME), FRAME)] = jnp.zeros(
                (INPUTS_DEV, FRAME), jnp.bfloat16
            )

    @pl.when(b > 0)
    def _():
        forward.wait_recv()

    pl.loop(0, 4)(lambda q: fir(0, q))
    back.wait_recv()
    pl.loop(0, 4)(lambda q: fir(7, q, True))

    @pl.loop(0, 2)
    def _(j):
        pl.loop(2, 4)(lambda quarter: dft(j, quarter))
        send(j, lambda other: outbox.at[j, other, high], inbox.at[j, a, b, high])

    @pl.loop(2, GROUPS)
    def _(j):
        pl.loop(0, QUARTERS)(lambda quarter: dft(j, quarter))

        @pl.when(j == 2)
        def _():
            send(2, lambda other: outbox.at[2, other], inbox.at[2, a, b])

        @pl.when(j == 3)
        def _():
            send(3, lambda other: outbox.at[3, other], last.at[a, b])

    owns = [
        pltpu.make_async_copy(
            outbox.at[j, me], inbox.at[j, a, b] if j < 3 else last.at[a, b], own_sems.at[j]
        )
        for j in range(GROUPS)
    ]
    for own in owns:
        own.start()

    back.wait_send()

    @pl.when(b < TM - 1)
    def _():
        forward.wait_send()

    def arrived(j):
        some = outbox.at[j, pl.ds(0, DEVICES - 1)]
        pltpu.make_async_copy(some, some, recv_sems.at[j]).wait()

    for j in range(3):
        owns[j].wait()

    @pl.loop(0, 3)
    def _(j):
        arrived(j)

        correlate_channel(inbox.at[j], rows, swapped, scale_col, scale_row, done.at[j])

    owns[3].wait()
    arrived(3)

    @pl.loop(0, GROUPS)
    def _(j):
        some = outbox.at[j, pl.ds(0, DEVICES - 1)]
        pltpu.make_async_copy(some, some, send_sems.at[j]).wait()


def channelize(voltages, prototype, table):
    piece = (INP, TM, QUARTERS, 2 * PAIRS, 128)
    return pl.pallas_call(
        channelize_kernel,
        out_shape=(
            pltpu.VMEM((3, 2, INPUTS, INPUTS), jnp.bfloat16),
            pltpu.VMEM(piece, jnp.bfloat16),
        ),
        in_specs=[
            pl.BlockSpec(memory_space=pl.ANY),
            pl.BlockSpec(memory_space=pltpu.VMEM),
            pl.BlockSpec(memory_space=pl.ANY),
        ],
        out_specs=(pl.BlockSpec(memory_space=pltpu.VMEM), pl.BlockSpec(memory_space=pltpu.VMEM)),
        scratch_shapes=[
            pltpu.VMEM((INPUTS_DEV, (SPEC_DEV + HALO) * FRAME), jnp.bfloat16),
            pltpu.VMEM((GROUPS, 2 * DEVICES, FRAME), jnp.bfloat16),
            pltpu.VMEM((SPEC_DEV, INPUTS_DEV, FRAME), jnp.bfloat16),
            pltpu.VMEM((2 * DEVICES * STRIDE, 128), jnp.float32),
            pltpu.VMEM((GROUPS, DEVICES, QUARTERS, 2 * PAIRS, 128), jnp.bfloat16),
            pltpu.VMEM((3, *piece), jnp.bfloat16),
            pltpu.VMEM((INPUTS, INPUTS), jnp.bfloat16),
            pltpu.VMEM((INPUTS, INPUTS), jnp.bfloat16),
            pltpu.VMEM((INPUTS, 128), jnp.float32),
            pltpu.VMEM((1, INPUTS), jnp.float32),
            pltpu.SemaphoreType.DMA((3,)),
            pltpu.SemaphoreType.DMA,
            pltpu.SemaphoreType.DMA((GROUPS,)),
            pltpu.SemaphoreType.DMA((4,)),
            pltpu.SemaphoreType.DMA((GROUPS,)),
            pltpu.SemaphoreType.DMA((GROUPS,)),
            pltpu.SemaphoreType.REGULAR,
        ],
        compiler_params=pltpu.CompilerParams(
            collective_id=0, has_side_effects=True, vmem_limit_bytes=43 * 1024 * 1024
        ),
        name="channelize",
    )(voltages, prototype, table)


def finish_kernel(done, last, o_hbm, rows, swapped, scale_col, scale_row, staged, sems):
    copies = [pltpu.make_async_copy(done.at[c], o_hbm.at[c], sems.at[c]) for c in range(3)]
    for copy in copies:
        copy.start()

    def finished(m):
        at = pl.ds(m * TILE, TILE if m < 2 else 2 * TILE)
        copies.append(
            pltpu.make_async_copy(staged.at[:, at], o_hbm.at[3, :, at], sems.at[3 + m])
        )
        copies[-1].start()

    correlate_channel(last, rows, swapped, scale_col, scale_row, staged, finished)
    for copy in copies:
        copy.wait()


def finish(done, last):
    return pl.pallas_call(
        finish_kernel,
        out_shape=jax.ShapeDtypeStruct((GROUPS, 2, INPUTS, INPUTS), jnp.bfloat16),
        in_specs=[pl.BlockSpec(memory_space=pltpu.VMEM)] * 2,
        out_specs=pl.BlockSpec(memory_space=pl.ANY),
        scratch_shapes=[
            pltpu.VMEM((INPUTS, INPUTS), jnp.bfloat16),
            pltpu.VMEM((INPUTS, INPUTS), jnp.bfloat16),
            pltpu.VMEM((INPUTS, 128), jnp.float32),
            pltpu.VMEM((1, INPUTS), jnp.float32),
            pltpu.VMEM((2, INPUTS, INPUTS), jnp.bfloat16),
            pltpu.SemaphoreType.DMA((6,)),
        ],
        compiler_params=pltpu.CompilerParams(vmem_limit_bytes=20 * 1024 * 1024),
        name="finish",
    )(done, last)


def shards(voltages, prototype):
    table = jnp.asarray(dft_rows())
    return finish(*channelize(voltages, prototype, table))


def solution(mesh):
    return jax.shard_map(
        shards,
        mesh=mesh,
        in_specs=(P("inp", "tm"), P()),
        out_specs=P(("inp", "tm"), None, None, None),
        check_vma=False,
    )
```

```python
import functools
import math

import jax
import jax.numpy as jnp
import numpy as np
from jax import lax
from jax.experimental import pallas as pl
from jax.experimental.pallas import tpu as pltpu
from jax.sharding import PartitionSpec as P

TAPS = 8
HALO = TAPS - 1
AFTER = HALO // 2
BEFORE = HALO - AFTER
FRAME = 1024
INPUTS = 1024
INPUTS_DEV = 64
SPEC_DEV = 64
DEVICES = 128
GROUPS = 4
INP = 16
TM = 8
QUARTERS = 4
QUARTER = SPEC_DEV // QUARTERS
PAIRS = QUARTER // 2
STRIDE = PAIRS + 1
TILE = 256
TILES = [(m, n) for m in range(INPUTS // TILE) for n in range(m, INPUTS // TILE)]
MESH = pl.DeviceIdType.MESH


def dft_rows():
    channel = np.arange(DEVICES)[None, :] * GROUPS + np.arange(GROUPS)[:, None]
    sample = np.arange(FRAME)
    phase = (channel[:, :, None] * sample % FRAME) * (2.0 * math.pi / FRAME)
    table = np.stack([np.cos(phase), -np.sin(phase)], axis=2)
    return table.reshape(GROUPS, 2 * DEVICES, FRAME).astype(jnp.bfloat16)


def correlate_channel(
    parts, rows, swapped, scale_col, scale_row, out, held=None, finished=None
):
    depth = INPUTS // 4
    width = 2 * depth * len(parts)

    @pl.loop(0, INP)
    def _(a):
        at = pl.ds(pl.multiple_of(a * INPUTS_DEV, INPUTS_DEV), INPUTS_DEV)
        for n, part in enumerate(parts):
            turned = part[a].reshape(depth, 128).T
            for h in range(2):
                base = (2 * n + h) * depth
                rows[at, base : base + depth] = turned[h * 64 : (h + 1) * 64]

    def grams(m, n):
        other = rows[n * TILE : (n + 1) * TILE, :width]
        dims = (((1,), (1,)), ((), ()))
        pair = [
            lax.dot_general(
                ref[m * TILE : (m + 1) * TILE, :width],
                other,
                dims,
                preferred_element_type=jnp.float32,
            )
            for ref in (rows, swapped)
        ]
        if out is None:
            for k in range(2):
                held[TILES.index((m, n)), k] = pair[k]
        elif held is not None:
            pair = [pair[k] + held[TILES.index((m, n)), k] for k in range(2)]
        return pair

    first = lax.rem(lax.broadcasted_iota(jnp.int32, (TILE, 128), 1), 2 * PAIRS) < PAIRS
    eye = lax.broadcasted_iota(jnp.int32, (TILE, TILE), 0) == lax.broadcasted_iota(
        jnp.int32, (TILE, TILE), 1
    )
    for m in range(INPUTS // TILE):
        at = slice(m * TILE, (m + 1) * TILE)
        for n in range(width // 128):
            to = slice(n * 128, (n + 1) * 128)
            some = rows[at, to]
            ahead = pltpu.roll(some, 128 - PAIRS, 1)
            swapped[at, to] = jnp.where(first, ahead, -pltpu.roll(some, PAIRS, 1))
        if out is None:
            continue
        real, imag = grams(m, m)
        diagonal = jnp.where(eye, real, 0.0)
        column = lax.rsqrt(jnp.sum(diagonal, axis=1, keepdims=True) + 1e-06)
        row = lax.rsqrt(jnp.sum(diagonal, axis=0, keepdims=True) + 1e-06)
        scale_col[at, :] = jnp.broadcast_to(column, (TILE, 128))
        scale_row[:, at] = row
        outer = column * row
        out[0, at, at] = (real * outer).astype(jnp.bfloat16)
        out[1, at, at] = (imag * outer).astype(jnp.bfloat16)
    if out is None:
        for m, n in TILES:
            grams(m, n)
        return
    for m in range(INPUTS // TILE - 1):
        at = slice(m * TILE, (m + 1) * TILE)
        column = scale_col[at, 0:1]
        for n in range(m + 1, INPUTS // TILE):
            to = slice(n * TILE, (n + 1) * TILE)
            outer = column * scale_row[:, to]
            real, imag = grams(m, n)
            real = (real * outer).astype(jnp.bfloat16)
            imag = (imag * outer).astype(jnp.bfloat16)
            out[0, at, to] = real
            out[1, at, to] = imag
            out[0, to, at] = real.T
            out[1, to, at] = -imag.T
        if finished is not None:
            finished(m)


def channelize_kernel(
    v_hbm, proto_ref, table_hbm, done, held, last,
    v, table, filtered, turned, outbox, inbox, early, rows, swapped, scale_col, scale_row,
    v_sems, table_sem, own_sems, halo_sems, send_sems, recv_sems, row_sem,
):
    a = lax.axis_index("inp")
    b = lax.axis_index("tm")
    me = a * TM + b
    barrier = pltpu.get_barrier_semaphore()

    def frames(first, count):
        return pl.ds(pl.multiple_of(first * FRAME, FRAME), count * FRAME)

    loads = [
        pltpu.make_async_copy(
            v_hbm.at[:, frames(first, count)], v.at[:, frames(BEFORE + first, count)], v_sems.at[n]
        )
        for n, (first, count) in enumerate(((12, 24), (36, 28), (0, 12)))
    ]
    for load in loads:
        load.start()
    table_load = pltpu.make_async_copy(table_hbm, table, table_sem)
    table_load.start()

    def place(k):
        other = lax.rem(me + k * 37, DEVICES)
        return other, {"inp": lax.div(other, TM), "tm": lax.rem(other, TM)}

    @pl.loop(1, INP)
    def _(k):
        pl.semaphore_signal(
            barrier, inc=1, device_id={"inp": lax.rem(a + k, INP)}, device_id_type=MESH
        )

    def signal_row(semaphore):
        @pl.loop(1, TM)
        def _(k):
            pl.semaphore_signal(
                semaphore, inc=1, device_id={"tm": lax.rem(b + k, TM)}, device_id_type=MESH
            )

    signal_row(barrier)

    def fir(chunk, q, last=False):
        at = pl.ds(pl.multiple_of(q * 16, 16), 16)
        slot = lax.rem(chunk + 6, 8) * 8
        keep = jnp.where(b < TM - 1, 1.0, 0.0) if last else None
        for nb in range(FRAME // 128):
            lanes = slice(nb * 128, (nb + 1) * 128)
            taps = [proto_ref[k : k + 1, lanes] for k in range(TAPS)]
            x = [
                v[
                    at, pl.ds(pl.multiple_of((chunk * 8 + f) * FRAME + nb * 128, 128), 128)
                ].astype(jnp.float32)
                for f in range(8 + HALO)
            ]
            for s in range(8):
                total = taps[0] * x[s]
                for k in range(1, TAPS):
                    if last and s + k == 8 + BEFORE:
                        total = total * keep
                    total = total + taps[k] * x[s + k]
                filtered[slot + s, at, lanes] = total.astype(jnp.bfloat16)

    def dft(j, quarter):
        block = filtered[pl.ds(quarter * QUARTER, QUARTER)].reshape(QUARTER * INPUTS_DEV, FRAME)
        out = lax.dot_general(
            table[j], block, (((1,), (1,)), ((), ())), preferred_element_type=jnp.float32
        )
        for l in range(PAIRS):
            turned[pl.ds(l, 2 * DEVICES, stride=STRIDE), :] = out[:, l * 128 : (l + 1) * 128]
        for d in range(DEVICES):
            parts = [turned[pl.ds((2 * d + p) * STRIDE, PAIRS), :] for p in range(2)]
            outbox[j, d, quarter] = jnp.concatenate(parts, axis=0).astype(jnp.bfloat16)

    def send(j, source, target, arrival=None):
        @pl.loop(1, DEVICES)
        def _(k):
            other, where = place(k)
            pltpu.make_async_remote_copy(
                src_ref=source(other),
                dst_ref=target,
                send_sem=send_sems.at[j],
                recv_sem=recv_sems.at[j if arrival is None else arrival],
                device_id=where,
                device_id_type=MESH,
            ).start()

    def halo(first, count, to, step, n):
        return pltpu.make_async_remote_copy(
            src_ref=v.at[:, frames(first, count)],
            dst_ref=v.at[:, frames(to, count)],
            send_sem=halo_sems.at[n],
            recv_sem=halo_sems.at[2 + n],
            device_id={"tm": lax.rem(b + step, TM)},
            device_id_type=MESH,
        )

    forward = halo(SPEC_DEV, BEFORE, 0, 1, 0)
    back = halo(BEFORE, AFTER, BEFORE + SPEC_DEV, TM - 1, 1)
    loads[0].wait()
    pl.loop(0, 4)(lambda q: fir(2, q))
    loads[1].wait()
    loads[2].wait()
    pl.semaphore_wait(barrier, INP + TM - 2)
    back.start()

    @pl.when(b < TM - 1)
    def _():
        forward.start()

    signal_row(row_sem)

    pl.loop(0, 4)(lambda q: fir(3, q))
    table_load.wait()
    pl.semaphore_wait(row_sem, TM - 1)

    @pl.loop(0, 2)
    def _(quarter):
        @pl.when(quarter == 1)
        def _():
            pl.loop(0, 8)(lambda t: fir(4 + lax.div(t, 4), lax.rem(t, 4)))

        dft(0, quarter)
        send(0, lambda other: outbox.at[0, other, quarter], inbox.at[0, a, b, quarter])

    low = pl.ds(0, 2)
    high = pl.ds(2, 2)
    pl.loop(0, 2)(lambda quarter: dft(1, quarter))
    send(1, lambda other: outbox.at[1, other, low], inbox.at[1, a, b, low])

    pl.loop(0, 8)(lambda t: fir(6 - 5 * lax.div(t, 4), lax.rem(t, 4)))

    @pl.when(b == 0)
    def _():
        @pl.loop(0, BEFORE)
        def _(f):
            v[:, pl.ds(pl.multiple_of(f * FRAME, FRAME), FRAME)] = jnp.zeros(
                (INPUTS_DEV, FRAME), jnp.bfloat16
            )

    @pl.when(b > 0)
    def _():
        forward.wait_recv()

    pl.loop(0, 4)(lambda q: fir(0, q))
    back.wait_recv()
    pl.loop(0, 4)(lambda q: fir(7, q, True))

    @pl.loop(0, 2)
    def _(j):
        pl.loop(2, 4)(lambda quarter: dft(j, quarter))
        send(j, lambda other: outbox.at[j, other, high], inbox.at[j, a, b, high])

    pl.loop(0, QUARTERS)(lambda quarter: dft(2, quarter))
    send(2, lambda other: outbox.at[2, other], inbox.at[2, a, b])

    @pl.loop(0, 2)
    def _(half):
        pl.loop(0, 2)(lambda n: dft(3, 2 * half + n))

        @pl.when(half == 0)
        def _():
            send(3, lambda other: outbox.at[3, other, low], early.at[a, b], 3)

        @pl.when(half == 1)
        def _():
            send(3, lambda other: outbox.at[3, other, high], last.at[a, b], 4)

    owns = [
        pltpu.make_async_copy(outbox.at[j, me], inbox.at[j, a, b], own_sems.at[j])
        for j in range(3)
    ] + [
        pltpu.make_async_copy(outbox.at[3, me, low], early.at[a, b], own_sems.at[3]),
        pltpu.make_async_copy(outbox.at[3, me, high], last.at[a, b], own_sems.at[4]),
    ]
    for own in owns:
        own.start()

    back.wait_send()

    @pl.when(b < TM - 1)
    def _():
        forward.wait_send()

    def arrived(j, some):
        pltpu.make_async_copy(some, some, recv_sems.at[j]).wait()

    for own in owns:
        own.wait()

    @pl.loop(0, 3)
    def _(j):
        arrived(j, outbox.at[j, pl.ds(0, DEVICES - 1)])
        box = inbox.at[j]
        halves = [box.at[:, :, low], box.at[:, :, high]]
        correlate_channel(halves, rows, swapped, scale_col, scale_row, done.at[j])

    arrived(3, outbox.at[3, pl.ds(0, DEVICES - 1), low])
    correlate_channel([early], rows, swapped, scale_col, scale_row, None, held)
    arrived(4, outbox.at[3, pl.ds(0, DEVICES - 1), high])

    @pl.loop(0, GROUPS)
    def _(j):
        some = outbox.at[j, pl.ds(0, DEVICES - 1)]
        pltpu.make_async_copy(some, some, send_sems.at[j]).wait()


def channelize(voltages, prototype, table):
    piece = (INP, TM, QUARTERS, 2 * PAIRS, 128)
    half = (INP, TM, 2, 2 * PAIRS, 128)
    return pl.pallas_call(
        channelize_kernel,
        out_shape=(
            pltpu.VMEM((3, 2, INPUTS, INPUTS), jnp.bfloat16),
            pltpu.VMEM((len(TILES), 2, TILE, TILE), jnp.float32),
            pltpu.VMEM(half, jnp.bfloat16),
        ),
        in_specs=[
            pl.BlockSpec(memory_space=pl.ANY),
            pl.BlockSpec(memory_space=pltpu.VMEM),
            pl.BlockSpec(memory_space=pl.ANY),
        ],
        out_specs=(pl.BlockSpec(memory_space=pltpu.VMEM),) * 3,
        scratch_shapes=[
            pltpu.VMEM((INPUTS_DEV, (SPEC_DEV + HALO) * FRAME), jnp.bfloat16),
            pltpu.VMEM((GROUPS, 2 * DEVICES, FRAME), jnp.bfloat16),
            pltpu.VMEM((SPEC_DEV, INPUTS_DEV, FRAME), jnp.bfloat16),
            pltpu.VMEM((2 * DEVICES * STRIDE, 128), jnp.float32),
            pltpu.VMEM((GROUPS, DEVICES, QUARTERS, 2 * PAIRS, 128), jnp.bfloat16),
            pltpu.VMEM((3, *piece), jnp.bfloat16),
            pltpu.VMEM(half, jnp.bfloat16),
            pltpu.VMEM((INPUTS, INPUTS), jnp.bfloat16),
            pltpu.VMEM((INPUTS, INPUTS), jnp.bfloat16),
            pltpu.VMEM((INPUTS, 128), jnp.float32),
            pltpu.VMEM((1, INPUTS), jnp.float32),
            pltpu.SemaphoreType.DMA((3,)),
            pltpu.SemaphoreType.DMA,
            pltpu.SemaphoreType.DMA((GROUPS + 1,)),
            pltpu.SemaphoreType.DMA((4,)),
            pltpu.SemaphoreType.DMA((GROUPS,)),
            pltpu.SemaphoreType.DMA((GROUPS + 1,)),
            pltpu.SemaphoreType.REGULAR,
        ],
        compiler_params=pltpu.CompilerParams(
            collective_id=0, has_side_effects=True, vmem_limit_bytes=44 * 1024 * 1024
        ),
        name="channelize",
    )(voltages, prototype, table)


def finish_kernel(done, held, last, o_hbm, rows, swapped, scale_col, scale_row, staged, sems):
    copies = [pltpu.make_async_copy(done.at[c], o_hbm.at[c], sems.at[c]) for c in range(3)]
    for copy in copies:
        copy.start()

    def finished(m):
        at = pl.ds(m * TILE, TILE if m < 2 else 2 * TILE)
        copies.append(
            pltpu.make_async_copy(staged.at[:, at], o_hbm.at[3, :, at], sems.at[3 + m])
        )
        copies[-1].start()

    correlate_channel([last], rows, swapped, scale_col, scale_row, staged, held, finished)
    for copy in copies:
        copy.wait()


def finish(done, held, last):
    return pl.pallas_call(
        finish_kernel,
        out_shape=jax.ShapeDtypeStruct((GROUPS, 2, INPUTS, INPUTS), jnp.bfloat16),
        in_specs=[pl.BlockSpec(memory_space=pltpu.VMEM)] * 3,
        out_specs=pl.BlockSpec(memory_space=pl.ANY),
        scratch_shapes=[
            pltpu.VMEM((INPUTS, INPUTS // 2), jnp.bfloat16),
            pltpu.VMEM((INPUTS, INPUTS // 2), jnp.bfloat16),
            pltpu.VMEM((INPUTS, 128), jnp.float32),
            pltpu.VMEM((1, INPUTS), jnp.float32),
            pltpu.VMEM((2, INPUTS, INPUTS), jnp.bfloat16),
            pltpu.SemaphoreType.DMA((6,)),
        ],
        compiler_params=pltpu.CompilerParams(vmem_limit_bytes=20 * 1024 * 1024),
        name="finish",
    )(done, held, last)


def shards(voltages, prototype):
    table = jnp.asarray(dft_rows())
    return finish(*channelize(voltages, prototype, table))


def solution(mesh):
    return jax.shard_map(
        shards,
        mesh=mesh,
        in_specs=(P("inp", "tm"), P()),
        out_specs=P(("inp", "tm"), None, None, None),
        check_vma=False,
    )
```

```python
import functools
import math

import jax
import jax.numpy as jnp
import numpy as np
from jax import lax
from jax.experimental import pallas as pl
from jax.experimental.pallas import tpu as pltpu
from jax.sharding import PartitionSpec as P

TAPS = 8
HALO = TAPS - 1
AFTER = HALO // 2
BEFORE = HALO - AFTER
FRAME = 1024
INPUTS = 1024
INPUTS_DEV = 64
SPEC_DEV = 64
DEVICES = 128
GROUPS = 4
INP = 16
TM = 8
QUARTERS = 4
QUARTER = SPEC_DEV // QUARTERS
PAIRS = QUARTER // 2
STRIDE = PAIRS + 1
TILE = 256
TILES = [(m, n) for m in range(INPUTS // TILE) for n in range(m, INPUTS // TILE)]
MESH = pl.DeviceIdType.MESH


def dft_rows():
    channel = np.arange(DEVICES)[None, :] * GROUPS + np.arange(GROUPS)[:, None]
    sample = np.arange(FRAME)
    phase = (channel[:, :, None] * sample % FRAME) * (2.0 * math.pi / FRAME)
    table = np.stack([np.cos(phase), -np.sin(phase)], axis=2)
    return table.reshape(GROUPS, 2 * DEVICES, FRAME).astype(jnp.bfloat16)


def correlate_channel(
    parts, rows, swapped, scale_col, scale_row, out, held=None, finished=None
):
    depth = INPUTS // 4
    width = 2 * depth * len(parts)

    @pl.loop(0, INP)
    def _(a):
        at = pl.ds(pl.multiple_of(a * INPUTS_DEV, INPUTS_DEV), INPUTS_DEV)
        for n, part in enumerate(parts):
            turned = part[a].reshape(depth, 128).T
            for h in range(2):
                base = (2 * n + h) * depth
                rows[at, base : base + depth] = turned[h * 64 : (h + 1) * 64]

    def grams(m, n):
        other = rows[n * TILE : (n + 1) * TILE, :width]
        dims = (((1,), (1,)), ((), ()))
        pair = [
            lax.dot_general(
                ref[m * TILE : (m + 1) * TILE, :width],
                other,
                dims,
                preferred_element_type=jnp.float32,
            )
            for ref in (rows, swapped)
        ]
        if out is None:
            for k in range(2):
                held[TILES.index((m, n)), k] = pair[k]
        elif held is not None:
            pair = [pair[k] + held[TILES.index((m, n)), k] for k in range(2)]
        return pair

    first = lax.rem(lax.broadcasted_iota(jnp.int32, (TILE, 128), 1), 2 * PAIRS) < PAIRS
    eye = lax.broadcasted_iota(jnp.int32, (TILE, TILE), 0) == lax.broadcasted_iota(
        jnp.int32, (TILE, TILE), 1
    )
    for m in range(INPUTS // TILE):
        at = slice(m * TILE, (m + 1) * TILE)
        for n in range(width // 128):
            to = slice(n * 128, (n + 1) * 128)
            some = rows[at, to]
            ahead = pltpu.roll(some, 128 - PAIRS, 1)
            swapped[at, to] = jnp.where(first, ahead, -pltpu.roll(some, PAIRS, 1))
        if out is None:
            continue
        real, imag = grams(m, m)
        diagonal = jnp.where(eye, real, 0.0)
        column = lax.rsqrt(jnp.sum(diagonal, axis=1, keepdims=True) + 1e-06)
        row = lax.rsqrt(jnp.sum(diagonal, axis=0, keepdims=True) + 1e-06)
        scale_col[at, :] = jnp.broadcast_to(column, (TILE, 128))
        scale_row[:, at] = row
        outer = column * row
        out[0, at, at] = (real * outer).astype(jnp.bfloat16)
        out[1, at, at] = (imag * outer).astype(jnp.bfloat16)
    if out is None:
        for m, n in TILES:
            grams(m, n)
        return
    for m in range(INPUTS // TILE - 1):
        at = slice(m * TILE, (m + 1) * TILE)
        column = scale_col[at, 0:1]
        for n in range(m + 1, INPUTS // TILE):
            to = slice(n * TILE, (n + 1) * TILE)
            outer = column * scale_row[:, to]
            real, imag = grams(m, n)
            real = (real * outer).astype(jnp.bfloat16)
            imag = (imag * outer).astype(jnp.bfloat16)
            out[0, at, to] = real
            out[1, at, to] = imag
            out[0, to, at] = real.T
            out[1, to, at] = -imag.T
        if finished is not None:
            finished(m)


def channelize_kernel(
    v_hbm, proto_ref, table_hbm, done, held, last,
    v, table, filtered, turned, outbox, inbox, early, rows, swapped, scale_col, scale_row,
    v_sems, table_sem, own_sems, halo_sems, send_sems, recv_sems, row_sem,
):
    a = lax.axis_index("inp")
    b = lax.axis_index("tm")
    me = a * TM + b
    barrier = pltpu.get_barrier_semaphore()

    def frames(first, count):
        return pl.ds(pl.multiple_of(first * FRAME, FRAME), count * FRAME)

    loads = [
        pltpu.make_async_copy(
            v_hbm.at[:, frames(first, count)], v.at[:, frames(BEFORE + first, count)], v_sems.at[n]
        )
        for n, (first, count) in enumerate(
            ((SPEC_DEV - BEFORE, BEFORE), (0, AFTER), (12, 24), (36, 24), (AFTER, 9))
        )
    ]
    for load in loads[:2]:
        load.start()

    def place(k):
        other = lax.rem(me + k * 37, DEVICES)
        return other, {"inp": lax.div(other, TM), "tm": lax.rem(other, TM)}

    @pl.loop(1, INP)
    def _(k):
        pl.semaphore_signal(
            barrier, inc=1, device_id={"inp": lax.rem(a + k, INP)}, device_id_type=MESH
        )

    def signal_row(semaphore):
        @pl.loop(1, TM)
        def _(k):
            pl.semaphore_signal(
                semaphore, inc=1, device_id={"tm": lax.rem(b + k, TM)}, device_id_type=MESH
            )

    signal_row(barrier)
    for load in loads[2:]:
        load.start()
    table_load = pltpu.make_async_copy(table_hbm, table, table_sem)
    table_load.start()

    def fir(chunk, q, last=False):
        at = pl.ds(pl.multiple_of(q * 16, 16), 16)
        slot = lax.rem(chunk + 6, 8) * 8
        keep = jnp.where(b < TM - 1, 1.0, 0.0) if last else None
        for nb in range(FRAME // 128):
            lanes = slice(nb * 128, (nb + 1) * 128)
            taps = [proto_ref[k : k + 1, lanes] for k in range(TAPS)]
            x = [
                v[
                    at, pl.ds(pl.multiple_of((chunk * 8 + f) * FRAME + nb * 128, 128), 128)
                ].astype(jnp.float32)
                for f in range(8 + HALO)
            ]
            for s in range(8):
                total = taps[0] * x[s]
                for k in range(1, TAPS):
                    if last and s + k == 8 + BEFORE:
                        total = total * keep
                    total = total + taps[k] * x[s + k]
                filtered[slot + s, at, lanes] = total.astype(jnp.bfloat16)

    def dft(j, quarter):
        block = filtered[pl.ds(quarter * QUARTER, QUARTER)].reshape(QUARTER * INPUTS_DEV, FRAME)
        out = lax.dot_general(
            table[j], block, (((1,), (1,)), ((), ())), preferred_element_type=jnp.float32
        )
        for l in range(PAIRS):
            turned[pl.ds(l, 2 * DEVICES, stride=STRIDE), :] = out[:, l * 128 : (l + 1) * 128]
        for d in range(DEVICES):
            parts = [turned[pl.ds((2 * d + p) * STRIDE, PAIRS), :] for p in range(2)]
            outbox[j, d, quarter] = jnp.concatenate(parts, axis=0).astype(jnp.bfloat16)

    def send(j, source, target, arrival=None):
        @pl.loop(1, DEVICES)
        def _(k):
            other, where = place(k)
            pltpu.make_async_remote_copy(
                src_ref=source(other),
                dst_ref=target,
                send_sem=send_sems.at[j],
                recv_sem=recv_sems.at[j if arrival is None else arrival],
                device_id=where,
                device_id_type=MESH,
            ).start()

    def halo(first, count, to, step, n):
        return pltpu.make_async_remote_copy(
            src_ref=v.at[:, frames(first, count)],
            dst_ref=v.at[:, frames(to, count)],
            send_sem=halo_sems.at[n],
            recv_sem=halo_sems.at[2 + n],
            device_id={"tm": lax.rem(b + step, TM)},
            device_id_type=MESH,
        )

    forward = halo(SPEC_DEV, BEFORE, 0, 1, 0)
    back = halo(BEFORE, AFTER, BEFORE + SPEC_DEV, TM - 1, 1)
    for load in loads[:2]:
        load.wait()
    pl.semaphore_wait(barrier, INP + TM - 2)
    back.start()

    @pl.when(b < TM - 1)
    def _():
        forward.start()

    signal_row(row_sem)
    loads[2].wait()
    pl.loop(0, 8)(lambda t: fir(2 + lax.div(t, 4), lax.rem(t, 4)))
    for load in loads[3:]:
        load.wait()
    table_load.wait()
    pl.semaphore_wait(row_sem, TM - 1)

    @pl.loop(0, 2)
    def _(quarter):
        @pl.when(quarter == 1)
        def _():
            pl.loop(0, 8)(lambda t: fir(4 + lax.div(t, 4), lax.rem(t, 4)))

        dft(0, quarter)
        send(0, lambda other: outbox.at[0, other, quarter], inbox.at[0, a, b, quarter])

    low = pl.ds(0, 2)
    high = pl.ds(2, 2)
    pl.loop(0, 2)(lambda quarter: dft(1, quarter))
    send(1, lambda other: outbox.at[1, other, low], inbox.at[1, a, b, low])

    pl.loop(0, 8)(lambda t: fir(6 - 5 * lax.div(t, 4), lax.rem(t, 4)))

    @pl.when(b == 0)
    def _():
        @pl.loop(0, BEFORE)
        def _(f):
            v[:, pl.ds(pl.multiple_of(f * FRAME, FRAME), FRAME)] = jnp.zeros(
                (INPUTS_DEV, FRAME), jnp.bfloat16
            )

    @pl.when(b > 0)
    def _():
        forward.wait_recv()

    pl.loop(0, 4)(lambda q: fir(0, q))
    back.wait_recv()
    pl.loop(0, 4)(lambda q: fir(7, q, True))

    @pl.loop(0, 2)
    def _(j):
        pl.loop(2, 4)(lambda quarter: dft(j, quarter))
        send(j, lambda other: outbox.at[j, other, high], inbox.at[j, a, b, high])

    pl.loop(0, QUARTERS)(lambda quarter: dft(2, quarter))
    send(2, lambda other: outbox.at[2, other], inbox.at[2, a, b])

    @pl.loop(0, 2)
    def _(half):
        pl.loop(0, 2)(lambda n: dft(3, 2 * half + n))

        @pl.when(half == 0)
        def _():
            send(3, lambda other: outbox.at[3, other, low], early.at[a, b], 3)

        @pl.when(half == 1)
        def _():
            send(3, lambda other: outbox.at[3, other, high], last.at[a, b], 4)

    owns = [
        pltpu.make_async_copy(outbox.at[j, me], inbox.at[j, a, b], own_sems.at[j])
        for j in range(3)
    ] + [
        pltpu.make_async_copy(outbox.at[3, me, low], early.at[a, b], own_sems.at[3]),
        pltpu.make_async_copy(outbox.at[3, me, high], last.at[a, b], own_sems.at[4]),
    ]
    for own in owns:
        own.start()

    back.wait_send()

    @pl.when(b < TM - 1)
    def _():
        forward.wait_send()

    def arrived(j, some):
        pltpu.make_async_copy(some, some, recv_sems.at[j]).wait()

    for own in owns:
        own.wait()

    @pl.loop(0, 3)
    def _(j):
        arrived(j, outbox.at[j, pl.ds(0, DEVICES - 1)])
        box = inbox.at[j]
        halves = [box.at[:, :, low], box.at[:, :, high]]
        correlate_channel(halves, rows, swapped, scale_col, scale_row, done.at[j])

    arrived(3, outbox.at[3, pl.ds(0, DEVICES - 1), low])
    correlate_channel([early], rows, swapped, scale_col, scale_row, None, held)
    arrived(4, outbox.at[3, pl.ds(0, DEVICES - 1), high])

    @pl.loop(0, GROUPS)
    def _(j):
        some = outbox.at[j, pl.ds(0, DEVICES - 1)]
        pltpu.make_async_copy(some, some, send_sems.at[j]).wait()


def channelize(voltages, prototype, table):
    piece = (INP, TM, QUARTERS, 2 * PAIRS, 128)
    half = (INP, TM, 2, 2 * PAIRS, 128)
    return pl.pallas_call(
        channelize_kernel,
        out_shape=(
            pltpu.VMEM((3, 2, INPUTS, INPUTS), jnp.bfloat16),
            pltpu.VMEM((len(TILES), 2, TILE, TILE), jnp.float32),
            pltpu.VMEM(half, jnp.bfloat16),
        ),
        in_specs=[
            pl.BlockSpec(memory_space=pl.ANY),
            pl.BlockSpec(memory_space=pltpu.VMEM),
            pl.BlockSpec(memory_space=pl.ANY),
        ],
        out_specs=(pl.BlockSpec(memory_space=pltpu.VMEM),) * 3,
        scratch_shapes=[
            pltpu.VMEM((INPUTS_DEV, (SPEC_DEV + HALO) * FRAME), jnp.bfloat16),
            pltpu.VMEM((GROUPS, 2 * DEVICES, FRAME), jnp.bfloat16),
            pltpu.VMEM((SPEC_DEV, INPUTS_DEV, FRAME), jnp.bfloat16),
            pltpu.VMEM((2 * DEVICES * STRIDE, 128), jnp.float32),
            pltpu.VMEM((GROUPS, DEVICES, QUARTERS, 2 * PAIRS, 128), jnp.bfloat16),
            pltpu.VMEM((3, *piece), jnp.bfloat16),
            pltpu.VMEM(half, jnp.bfloat16),
            pltpu.VMEM((INPUTS, INPUTS), jnp.bfloat16),
            pltpu.VMEM((INPUTS, INPUTS), jnp.bfloat16),
            pltpu.VMEM((INPUTS, 128), jnp.float32),
            pltpu.VMEM((1, INPUTS), jnp.float32),
            pltpu.SemaphoreType.DMA((5,)),
            pltpu.SemaphoreType.DMA,
            pltpu.SemaphoreType.DMA((GROUPS + 1,)),
            pltpu.SemaphoreType.DMA((4,)),
            pltpu.SemaphoreType.DMA((GROUPS,)),
            pltpu.SemaphoreType.DMA((GROUPS + 1,)),
            pltpu.SemaphoreType.REGULAR,
        ],
        compiler_params=pltpu.CompilerParams(
            collective_id=0, has_side_effects=True, vmem_limit_bytes=44 * 1024 * 1024
        ),
        name="channelize",
    )(voltages, prototype, table)


def finish_kernel(done, held, last, o_hbm, rows, swapped, scale_col, scale_row, staged, sems):
    copies = [pltpu.make_async_copy(done.at[c], o_hbm.at[c], sems.at[c]) for c in range(3)]
    for copy in copies:
        copy.start()

    def finished(m):
        at = pl.ds(m * TILE, TILE if m < 2 else 2 * TILE)
        copies.append(
            pltpu.make_async_copy(staged.at[:, at], o_hbm.at[3, :, at], sems.at[3 + m])
        )
        copies[-1].start()

    correlate_channel([last], rows, swapped, scale_col, scale_row, staged, held, finished)
    for copy in copies:
        copy.wait()


def finish(done, held, last):
    return pl.pallas_call(
        finish_kernel,
        out_shape=jax.ShapeDtypeStruct((GROUPS, 2, INPUTS, INPUTS), jnp.bfloat16),
        in_specs=[pl.BlockSpec(memory_space=pltpu.VMEM)] * 3,
        out_specs=pl.BlockSpec(memory_space=pl.ANY),
        scratch_shapes=[
            pltpu.VMEM((INPUTS, INPUTS // 2), jnp.bfloat16),
            pltpu.VMEM((INPUTS, INPUTS // 2), jnp.bfloat16),
            pltpu.VMEM((INPUTS, 128), jnp.float32),
            pltpu.VMEM((1, INPUTS), jnp.float32),
            pltpu.VMEM((2, INPUTS, INPUTS), jnp.bfloat16),
            pltpu.SemaphoreType.DMA((6,)),
        ],
        compiler_params=pltpu.CompilerParams(vmem_limit_bytes=20 * 1024 * 1024),
        name="finish",
    )(done, held, last)


def shards(voltages, prototype):
    table = jnp.asarray(dft_rows())
    return finish(*channelize(voltages, prototype, table))


def solution(mesh):
    return jax.shard_map(
        shards,
        mesh=mesh,
        in_specs=(P("inp", "tm"), P()),
        out_specs=P(("inp", "tm"), None, None, None),
        check_vma=False,
    )
```

```python
import functools
import math

import jax
import jax.numpy as jnp
import numpy as np
from jax import lax
from jax.experimental import pallas as pl
from jax.experimental.pallas import tpu as pltpu
from jax.sharding import PartitionSpec as P

TAPS = 8
HALO = TAPS - 1
AFTER = HALO // 2
BEFORE = HALO - AFTER
FRAME = 1024
INPUTS = 1024
INPUTS_DEV = 64
SPEC_DEV = 64
DEVICES = 128
GROUPS = 4
INP = 16
TM = 8
QUARTERS = 4
QUARTER = SPEC_DEV // QUARTERS
PAIRS = QUARTER // 2
STRIDE = PAIRS + 1
TILE = 256
TILES = [(m, n) for m in range(INPUTS // TILE) for n in range(m, INPUTS // TILE)]
MESH = pl.DeviceIdType.MESH


def dft_rows():
    channel = np.arange(DEVICES)[None, :] * GROUPS + np.arange(GROUPS)[:, None]
    sample = np.arange(FRAME)
    phase = (channel[:, :, None] * sample % FRAME) * (2.0 * math.pi / FRAME)
    table = np.stack([np.cos(phase), -np.sin(phase)], axis=2)
    return table.reshape(GROUPS, 2 * DEVICES, FRAME).astype(jnp.bfloat16)


def correlate_channel(
    parts, rows, swapped, scale_col, scale_row, out, held=None, finished=None
):
    depth = INPUTS // 4
    width = 2 * depth * len(parts)

    @pl.loop(0, INP)
    def _(a):
        at = pl.ds(pl.multiple_of(a * INPUTS_DEV, INPUTS_DEV), INPUTS_DEV)
        for n, part in enumerate(parts):
            turned = part[a].reshape(depth, 128).T
            for h in range(2):
                base = (2 * n + h) * depth
                rows[at, base : base + depth] = turned[h * 64 : (h + 1) * 64]

    def grams(m, n):
        other = rows[n * TILE : (n + 1) * TILE, :width]
        dims = (((1,), (1,)), ((), ()))
        pair = [
            lax.dot_general(
                ref[m * TILE : (m + 1) * TILE, :width],
                other,
                dims,
                preferred_element_type=jnp.float32,
            )
            for ref in (rows, swapped)
        ]
        if out is None:
            for k in range(2):
                held[TILES.index((m, n)), k] = pair[k]
        elif held is not None:
            pair = [pair[k] + held[TILES.index((m, n)), k] for k in range(2)]
        return pair

    first = lax.rem(lax.broadcasted_iota(jnp.int32, (TILE, 128), 1), 2 * PAIRS) < PAIRS
    eye = lax.broadcasted_iota(jnp.int32, (TILE, TILE), 0) == lax.broadcasted_iota(
        jnp.int32, (TILE, TILE), 1
    )
    for m in range(INPUTS // TILE):
        at = slice(m * TILE, (m + 1) * TILE)
        for n in range(width // 128):
            to = slice(n * 128, (n + 1) * 128)
            some = rows[at, to]
            ahead = pltpu.roll(some, 128 - PAIRS, 1)
            swapped[at, to] = jnp.where(first, ahead, -pltpu.roll(some, PAIRS, 1))
        if out is None:
            continue
        real, imag = grams(m, m)
        diagonal = jnp.where(eye, real, 0.0)
        column = lax.rsqrt(jnp.sum(diagonal, axis=1, keepdims=True) + 1e-06)
        row = lax.rsqrt(jnp.sum(diagonal, axis=0, keepdims=True) + 1e-06)
        scale_col[at, :] = jnp.broadcast_to(column, (TILE, 128))
        scale_row[:, at] = row
        outer = column * row
        out[0, at, at] = (real * outer).astype(jnp.bfloat16)
        out[1, at, at] = (imag * outer).astype(jnp.bfloat16)
    if out is None:
        for m, n in TILES:
            grams(m, n)
        return
    for m in range(INPUTS // TILE - 1):
        at = slice(m * TILE, (m + 1) * TILE)
        column = scale_col[at, 0:1]
        for n in range(m + 1, INPUTS // TILE):
            to = slice(n * TILE, (n + 1) * TILE)
            outer = column * scale_row[:, to]
            real, imag = grams(m, n)
            real = (real * outer).astype(jnp.bfloat16)
            imag = (imag * outer).astype(jnp.bfloat16)
            out[0, at, to] = real
            out[1, at, to] = imag
            out[0, to, at] = real.T
            out[1, to, at] = -imag.T
        if finished is not None:
            finished(m)


def channelize_kernel(
    v_hbm, proto_ref, table_hbm, done, held, last,
    v, table, filtered, turned, outbox, inbox, early, rows, swapped, scale_col, scale_row,
    v_sems, table_sem, own_sems, halo_sems, send_sems, recv_sems, row_sem,
):
    a = lax.axis_index("inp")
    b = lax.axis_index("tm")
    me = a * TM + b
    barrier = pltpu.get_barrier_semaphore()

    def frames(first, count):
        return pl.ds(pl.multiple_of(first * FRAME, FRAME), count * FRAME)

    loads = [
        pltpu.make_async_copy(
            v_hbm.at[:, frames(first, count)], v.at[:, frames(BEFORE + first, count)], v_sems.at[n]
        )
        for n, (first, count) in enumerate(
            ((SPEC_DEV - BEFORE, BEFORE), (0, AFTER), (12, 24), (36, 24), (AFTER, 9))
        )
    ]
    for load in loads[:2]:
        load.start()

    def place(k):
        other = lax.rem(me + k * 37, DEVICES)
        return other, {"inp": lax.div(other, TM), "tm": lax.rem(other, TM)}

    @pl.loop(1, INP)
    def _(k):
        pl.semaphore_signal(
            barrier, inc=1, device_id={"inp": lax.rem(a + k, INP)}, device_id_type=MESH
        )

    def signal_row(semaphore):
        @pl.loop(1, TM)
        def _(k):
            pl.semaphore_signal(
                semaphore, inc=1, device_id={"tm": lax.rem(b + k, TM)}, device_id_type=MESH
            )

    signal_row(barrier)
    for load in loads[2:]:
        load.start()
    table_load = pltpu.make_async_copy(table_hbm, table, table_sem)
    table_load.start()

    def fir(chunk, q, last=False):
        at = pl.ds(pl.multiple_of(q * 16, 16), 16)
        slot = lax.rem(chunk + 6, 8) * 8
        keep = jnp.where(b < TM - 1, 1.0, 0.0) if last else None
        for nb in range(FRAME // 128):
            lanes = slice(nb * 128, (nb + 1) * 128)
            taps = [proto_ref[k : k + 1, lanes] for k in range(TAPS)]
            x = [
                v[
                    at, pl.ds(pl.multiple_of((chunk * 8 + f) * FRAME + nb * 128, 128), 128)
                ].astype(jnp.float32)
                for f in range(8 + HALO)
            ]
            for s in range(8):
                total = taps[0] * x[s]
                for k in range(1, TAPS):
                    if last and s + k == 8 + BEFORE:
                        total = total * keep
                    total = total + taps[k] * x[s + k]
                filtered[slot + s, at, lanes] = total.astype(jnp.bfloat16)

    def dft(j, quarter):
        block = filtered[pl.ds(quarter * QUARTER, QUARTER)].reshape(QUARTER * INPUTS_DEV, FRAME)
        out = lax.dot_general(
            table[j], block, (((1,), (1,)), ((), ())), preferred_element_type=jnp.float32
        )
        for l in range(PAIRS):
            turned[pl.ds(l, 2 * DEVICES, stride=STRIDE), :] = out[:, l * 128 : (l + 1) * 128]
        for d in range(DEVICES):
            parts = [turned[pl.ds((2 * d + p) * STRIDE, PAIRS), :] for p in range(2)]
            outbox[j, d, quarter] = jnp.concatenate(parts, axis=0).astype(jnp.bfloat16)

    def send(j, source, target, arrival=None):
        @pl.loop(1, DEVICES)
        def _(k):
            other, where = place(k)
            pltpu.make_async_remote_copy(
                src_ref=source(other),
                dst_ref=target,
                send_sem=send_sems.at[j],
                recv_sem=recv_sems.at[j if arrival is None else arrival],
                device_id=where,
                device_id_type=MESH,
            ).start()

    def halo(first, count, to, step, n):
        return pltpu.make_async_remote_copy(
            src_ref=v.at[:, frames(first, count)],
            dst_ref=v.at[:, frames(to, count)],
            send_sem=halo_sems.at[n],
            recv_sem=halo_sems.at[2 + n],
            device_id={"tm": lax.rem(b + step, TM)},
            device_id_type=MESH,
        )

    forward = halo(SPEC_DEV, BEFORE, 0, 1, 0)
    back = halo(BEFORE, AFTER, BEFORE + SPEC_DEV, TM - 1, 1)
    for load in loads[:2]:
        load.wait()
    pl.semaphore_wait(barrier, INP + TM - 2)
    back.start()

    @pl.when(b < TM - 1)
    def _():
        forward.start()

    signal_row(row_sem)
    loads[2].wait()
    pl.loop(0, 8)(lambda t: fir(2 + lax.div(t, 4), lax.rem(t, 4)))
    for load in loads[3:]:
        load.wait()
    table_load.wait()
    pl.semaphore_wait(row_sem, TM - 1)

    @pl.loop(0, 2)
    def _(quarter):
        @pl.when(quarter == 1)
        def _():
            pl.loop(0, 8)(lambda t: fir(4 + lax.div(t, 4), lax.rem(t, 4)))

        dft(0, quarter)
        send(0, lambda other: outbox.at[0, other, quarter], inbox.at[0, a, b, quarter])

    low = pl.ds(0, 2)
    high = pl.ds(2, 2)
    pl.loop(0, 2)(lambda quarter: dft(1, quarter))
    send(1, lambda other: outbox.at[1, other, low], inbox.at[1, a, b, low])

    pl.loop(0, 8)(lambda t: fir(6 - 5 * lax.div(t, 4), lax.rem(t, 4)))

    @pl.when(b == 0)
    def _():
        @pl.loop(0, BEFORE)
        def _(f):
            v[:, pl.ds(pl.multiple_of(f * FRAME, FRAME), FRAME)] = jnp.zeros(
                (INPUTS_DEV, FRAME), jnp.bfloat16
            )

    @pl.when(b > 0)
    def _():
        forward.wait_recv()

    pl.loop(0, 4)(lambda q: fir(0, q))
    back.wait_recv()
    pl.loop(0, 4)(lambda q: fir(7, q, True))

    @pl.loop(0, 2)
    def _(j):
        pl.loop(2, 4)(lambda quarter: dft(j, quarter))
        send(j, lambda other: outbox.at[j, other, high], inbox.at[j, a, b, high])

    pl.loop(0, QUARTERS)(lambda quarter: dft(2, quarter))
    send(2, lambda other: outbox.at[2, other], inbox.at[2, a, b])

    @pl.loop(0, 2)
    def _(half):
        pl.loop(0, 2)(lambda n: dft(3, 2 * half + n))

        @pl.when(half == 0)
        def _():
            send(3, lambda other: outbox.at[3, other, low], early.at[a, b], 3)

        @pl.when(half == 1)
        def _():
            send(3, lambda other: outbox.at[3, other, high], last.at[a, b], 4)

    owns = [
        pltpu.make_async_copy(outbox.at[j, me], inbox.at[j, a, b], own_sems.at[j])
        for j in range(3)
    ] + [
        pltpu.make_async_copy(outbox.at[3, me, low], early.at[a, b], own_sems.at[3]),
        pltpu.make_async_copy(outbox.at[3, me, high], last.at[a, b], own_sems.at[4]),
    ]
    for own in owns:
        own.start()

    back.wait_send()

    @pl.when(b < TM - 1)
    def _():
        forward.wait_send()

    def arrived(j, some):
        pltpu.make_async_copy(some, some, recv_sems.at[j]).wait()

    for own in owns:
        own.wait()

    @pl.loop(0, 3)
    def _(j):
        arrived(j, outbox.at[j, pl.ds(0, DEVICES - 1)])
        box = inbox.at[j]
        halves = [box.at[:, :, low], box.at[:, :, high]]
        correlate_channel(halves, rows, swapped, scale_col, scale_row, done.at[j])

    arrived(3, outbox.at[3, pl.ds(0, DEVICES - 1), low])
    correlate_channel([early], rows, swapped, scale_col, scale_row, None, held)
    arrived(4, outbox.at[3, pl.ds(0, DEVICES - 1), high])

    @pl.loop(0, GROUPS)
    def _(j):
        some = outbox.at[j, pl.ds(0, DEVICES - 1)]
        pltpu.make_async_copy(some, some, send_sems.at[j]).wait()


def channelize(voltages, prototype, table):
    piece = (INP, TM, QUARTERS, 2 * PAIRS, 128)
    half = (INP, TM, 2, 2 * PAIRS, 128)
    return pl.pallas_call(
        channelize_kernel,
        out_shape=(
            pltpu.VMEM((3, 2, INPUTS, INPUTS), jnp.bfloat16),
            pltpu.VMEM((len(TILES), 2, TILE, TILE), jnp.float32),
            pltpu.VMEM(half, jnp.bfloat16),
        ),
        in_specs=[
            pl.BlockSpec(memory_space=pl.ANY),
            pl.BlockSpec(memory_space=pltpu.VMEM),
            pl.BlockSpec(memory_space=pl.ANY),
        ],
        out_specs=(pl.BlockSpec(memory_space=pltpu.VMEM),) * 3,
        scratch_shapes=[
            pltpu.VMEM((INPUTS_DEV, (SPEC_DEV + HALO) * FRAME), jnp.bfloat16),
            pltpu.VMEM((GROUPS, 2 * DEVICES, FRAME), jnp.bfloat16),
            pltpu.VMEM((SPEC_DEV, INPUTS_DEV, FRAME), jnp.bfloat16),
            pltpu.VMEM((2 * DEVICES * STRIDE + 16, 128), jnp.float32),
            pltpu.VMEM((GROUPS, DEVICES, QUARTERS, 2 * PAIRS, 128), jnp.bfloat16),
            pltpu.VMEM((3, *piece), jnp.bfloat16),
            pltpu.VMEM(half, jnp.bfloat16),
            pltpu.VMEM((INPUTS, INPUTS), jnp.bfloat16),
            pltpu.VMEM((INPUTS, INPUTS), jnp.bfloat16),
            pltpu.VMEM((INPUTS, 128), jnp.float32),
            pltpu.VMEM((1, INPUTS), jnp.float32),
            pltpu.SemaphoreType.DMA((5,)),
            pltpu.SemaphoreType.DMA,
            pltpu.SemaphoreType.DMA((GROUPS + 1,)),
            pltpu.SemaphoreType.DMA((4,)),
            pltpu.SemaphoreType.DMA((GROUPS,)),
            pltpu.SemaphoreType.DMA((GROUPS + 1,)),
            pltpu.SemaphoreType.REGULAR,
        ],
        compiler_params=pltpu.CompilerParams(
            collective_id=0, has_side_effects=True, vmem_limit_bytes=44 * 1024 * 1024
        ),
        name="channelize",
    )(voltages, prototype, table)


def finish_kernel(done, held, last, o_hbm, rows, swapped, scale_col, scale_row, staged, sems):
    copies = [pltpu.make_async_copy(done.at[c], o_hbm.at[c], sems.at[c]) for c in range(3)]
    for copy in copies:
        copy.start()

    def finished(m):
        at = pl.ds(m * TILE, TILE if m < 2 else 2 * TILE)
        copies.append(
            pltpu.make_async_copy(staged.at[:, at], o_hbm.at[3, :, at], sems.at[3 + m])
        )
        copies[-1].start()

    correlate_channel([last], rows, swapped, scale_col, scale_row, staged, held, finished)
    for copy in copies:
        copy.wait()


def finish(done, held, last):
    return pl.pallas_call(
        finish_kernel,
        out_shape=jax.ShapeDtypeStruct((GROUPS, 2, INPUTS, INPUTS), jnp.bfloat16),
        in_specs=[pl.BlockSpec(memory_space=pltpu.VMEM)] * 3,
        out_specs=pl.BlockSpec(memory_space=pl.ANY),
        scratch_shapes=[
            pltpu.VMEM((INPUTS, INPUTS // 2), jnp.bfloat16),
            pltpu.VMEM((INPUTS, INPUTS // 2), jnp.bfloat16),
            pltpu.VMEM((INPUTS, 128), jnp.float32),
            pltpu.VMEM((1, INPUTS), jnp.float32),
            pltpu.VMEM((2, INPUTS, INPUTS), jnp.bfloat16),
            pltpu.SemaphoreType.DMA((6,)),
        ],
        compiler_params=pltpu.CompilerParams(vmem_limit_bytes=20 * 1024 * 1024),
        name="finish",
    )(done, held, last)


def shards(voltages, prototype):
    table = jnp.asarray(dft_rows())
    return finish(*channelize(voltages, prototype, table))


def solution(mesh):
    return jax.shard_map(
        shards,
        mesh=mesh,
        in_specs=(P("inp", "tm"), P()),
        out_specs=P(("inp", "tm"), None, None, None),
        check_vma=False,
    )
```
